256 devices in a mesh: expert: 4 (over y_lo, core), row: 8 (over y_hi, x), col: 8 (over z).
Axes of the slice: x: 4, y: 4 (y_hi: 2, y_lo: 2; y = y_hi * 2 + y_lo), z: 8, core: 2. Of those that a mesh axis runs over, the one named last changes fastest.
Arguments:
- tokens: bfloat16 [512, 2880], P(('expert', 'row'), 'col'), may hold values from -6 to 6
- cotangent: bfloat16 [512, 2880], P(('expert', 'row'), 'col'), may hold values from -6 to 6
- w_gate: bfloat16 [16, 2880, 2880], P('expert', 'col', 'row'), may hold values from -0.109375 to 0.109375
- w_up: bfloat16 [16, 2880, 2880], P('expert', 'col', 'row'), may hold values from -0.109375 to 0.109375
- w_down: bfloat16 [16, 2880, 2880], P('expert', 'row', 'col'), may hold values from -0.109375 to 0.109375
- expert_ids: int32 [512, 4], P(('expert', 'row')), may hold values from 0 to 15, all different within a row; in each aligned block of 16 rows (0 to 15, 16 to 31, ...) at most 8 rows name the same one
- gates: float32 [512, 4], P(('expert', 'row')), may hold values from 0.05 to 1
Outputs:
- mixed: bfloat16 [512, 2880], P(('expert', 'row'), 'col')
- d_tokens: bfloat16 [512, 2880], P(('expert', 'row'), 'col')
- d_gates: float32 [512, 4], P(('expert', 'row'))
- grad_gate: bfloat16 [16, 2880, 2880], P('expert', 'col', 'row')
- grad_up: bfloat16 [16, 2880, 2880], P('expert', 'col', 'row')
- grad_down: bfloat16 [16, 2880, 2880], P('expert', 'row', 'col')
The draws below stay inside these ranges and needn't reach their ends.
Inputs may be any that keep to these rules, and one draw needn't show every extreme that they name: `expert_ids`: the 4 experts of a token are distinct. Within one token block of 16 consecutive tokens no expert is chosen by more than 8 pairs, and some expert is chosen by exactly 8 pairs in some blocks.
All inputs are finite; a program needn't handle non-finite values.
Results may differ from the reference program's by a relative error of at most 0.0058.
Values may be sent and summed in bfloat16 or wider, within the bound.
No kernel may reach another device: no remote copies, remote signals or barrier semaphores. Data moves between devices by JAX's collectives and lax.ppermute only.
A program may use at most 128 MiB of HBM per device.

```python
import math
import jax
import jax.numpy as jnp
import numpy as np
from jax import lax

D = 2880
FF = 2880
TOPK = 4
TOK_SRC = 16
EXPERTS = 16
CAP = 8
TOKENS = 512


def block_levels(key, shape, split, smallest, top_value):
    gain, own = 1.0, jax.random.fold_in(key, 6)
    for axis_at, shards_of in split:
        draws = jnp.exp(jax.random.uniform(jax.random.fold_in(own, axis_at), (shards_of,), jnp.float32, smallest / len(split), top_value / len(split)))
        gain = gain * jnp.repeat(draws, shape[axis_at] // shards_of).reshape([-1 if axis == axis_at else 1 for axis in range(len(shape))])
    return gain


def routed_block(stream_key, own, number, rows, count, top, reach, lean):
    sequence = jax.random.permutation(stream_key, count)
    crowded, usual = portions_of(count, rows * top, reach, lean, True), portions_of(count, rows * top, reach, lean, False)
    places = jnp.arange(count)

    def named(sizes, offset_by):
        used = int((sizes > 0).sum())
        fixed = max(1, used // 4)
        passed = fixed + (places - fixed + offset_by * (used - fixed)) % max(1, count - fixed)
        return jnp.zeros((count,), jnp.int32).at[sequence[jnp.where(places < fixed, places, passed)]].set(jnp.asarray(sizes, jnp.int32))

    sizes = jnp.where(number % 4 == 0, named(crowded, number // 4), named(usual, number - number // 4 - 1))
    mixed = jax.random.permutation(jax.random.fold_in(own, 3), count)
    source_of, sink = mixed[0:count // 2 * 2:2], mixed[1:count // 2 * 2:2]
    margin = jnp.minimum(sizes[source_of] - 1, reach - sizes[sink]) // 2
    margin = jnp.where((source_of == sequence[0]) | (sink == sequence[0]) | (sizes[sink] == 0), 0, jnp.maximum(margin, 0))
    passed = jax.random.randint(jax.random.fold_in(own, 4), (count // 2,), 0, 1 << 20) % (margin + 1)
    sizes = sizes.at[source_of].add(-passed).at[sink].add(passed)
    members = jnp.searchsorted(jnp.cumsum(sizes), jnp.arange(rows * top), side="right").astype(jnp.int32)
    listing = members.reshape(top, rows).T
    listing = listing[jax.random.permutation(jax.random.fold_in(own, 1), rows)]
    offset_by = jax.random.randint(jax.random.fold_in(own, 2), (rows, 1), 0, top)
    return jnp.take_along_axis(listing, (jnp.arange(top)[None, :] + offset_by) % top, axis=1)


def portions_of(number_of, total, reach, lean, full):
    portions = [(1 << 20) // math.isqrt(rank ** lean) + 1 for rank in range(1, number_of + 1)]
    largest = reach if full else min(reach, max(-(-total // number_of), total * portions[0] // sum(portions)))
    least = 1 if total - largest >= number_of - 1 else 0
    given, spare = [largest] + [least] * (number_of - 1), total - largest - least * (number_of - 1)
    while spare > 0:
        candidates = [i for i in range(1, number_of) if given[i] < largest] or [i for i in range(1, number_of) if given[i] < reach]
        pool, budget = sum([portions[i] for i in candidates]), spare
        for i in candidates:
            more = min(reach - given[i], max(1, budget * portions[i] // pool), spare)
            given[i] = given[i] + more
            spare = spare - more
    return np.array(given)


def centred(key, dims, deviation, limit, shards=(), kind=jnp.bfloat16):
    array = jax.random.normal(key, dims, jnp.float32) * deviation
    if len(shards) > 0:
        array = block_levels(key, dims, shards, -0.22, 0.18) * array
    return jnp.clip(array, min=-limit, max=limit).astype(kind)


def setup_inputs(seed: int = 0) -> dict:
    arg_keys = jax.random.split(jax.random.key(seed), 8)
    tokens = centred(arg_keys[0], (TOKENS, D), 1.0, 6.0, ((0, 32), (1, 8)))
    cotangent = centred(arg_keys[1], (TOKENS, D), 1.0, 6.0, ((0, 32), (1, 8)))
    w_gate = centred(arg_keys[2], (EXPERTS, D, FF), D ** -0.5, 0.109375, ((0, 4), (1, 8), (2, 8)))
    w_up = centred(arg_keys[3], (EXPERTS, D, FF), D ** -0.5, 0.109375, ((0, 4), (1, 8), (2, 8)))
    w_down = centred(arg_keys[4], (EXPERTS, FF, D), FF ** -0.5, 0.109375, ((0, 4), (1, 8), (2, 8)))
    expert_ids_keys = jax.random.split(jax.random.fold_in(arg_keys[5], 1), TOKENS // TOK_SRC)
    expert_ids_turns = jax.random.permutation(jax.random.fold_in(arg_keys[5], 3), TOKENS // TOK_SRC)
    expert_ids = jax.vmap(lambda own, number: routed_block(jax.random.fold_in(arg_keys[5], 2), own, number, TOK_SRC, EXPERTS, TOPK, CAP, 1))(expert_ids_keys, expert_ids_turns).reshape((TOKENS, TOPK))
    gates = jnp.clip(jnp.exp(math.log(1.0) - 2.9957323 * jax.random.uniform(arg_keys[6], (TOKENS, TOPK), jnp.float32) ** block_levels(arg_keys[6], (TOKENS, TOPK), ((0, 32),), -0.2, 0.2)), 0.05, 1.0)
    return dict(tokens=tokens, cotangent=cotangent, w_gate=w_gate, w_up=w_up, w_down=w_down, expert_ids=expert_ids, gates=gates)


def expert_pass(operands):
    x_rows, dy_rows, weight_gate, weight_up, weight_down = operands
    gate_pre = jnp.dot(x_rows, weight_gate, preferred_element_type=jnp.float32)
    up_pre = jnp.dot(x_rows, weight_up, preferred_element_type=jnp.float32)
    sigma_gate = jax.nn.sigmoid(gate_pre)
    hidden = (gate_pre * sigma_gate * up_pre).astype(jnp.bfloat16)
    y_rows = jnp.dot(hidden, weight_down, preferred_element_type=jnp.float32).astype(jnp.bfloat16)
    grad_hidden = jnp.dot(dy_rows, weight_down.astype(jnp.float32).T, precision=lax.Precision.HIGHEST)
    grad_gate_pre = (grad_hidden * up_pre * sigma_gate * (1.0 + gate_pre * (1.0 - sigma_gate))).astype(jnp.bfloat16)
    grad_up_pre = (grad_hidden * gate_pre * sigma_gate).astype(jnp.bfloat16)
    dx_rows = (jnp.dot(grad_gate_pre, weight_gate.T, preferred_element_type=jnp.float32)
               + jnp.dot(grad_up_pre, weight_up.T, preferred_element_type=jnp.float32)).astype(jnp.bfloat16)
    grad_wg = jnp.dot(x_rows.T, grad_gate_pre, preferred_element_type=jnp.float32).astype(jnp.bfloat16)
    grad_wu = jnp.dot(x_rows.T, grad_up_pre, preferred_element_type=jnp.float32).astype(jnp.bfloat16)
    grad_wd = jnp.dot(hidden.astype(jnp.float32).T, dy_rows, precision=lax.Precision.HIGHEST).astype(jnp.bfloat16)
    return y_rows, dx_rows, grad_wg, grad_wu, grad_wd


def reference(tokens, cotangent, w_gate, w_up, w_down, expert_ids, gates):
    blocks = TOKENS // TOK_SRC
    pairs = TOK_SRC * TOPK
    block_ids = expert_ids.reshape(blocks, pairs)
    onehot = (block_ids[:, :, None] == jnp.arange(EXPERTS, dtype=jnp.int32)[None, None, :]).astype(jnp.int32)
    slot = jnp.sum((jnp.cumsum(onehot, axis=1) - onehot) * onehot, axis=2).astype(jnp.int32)
    block_index = jnp.broadcast_to(jnp.arange(blocks, dtype=jnp.int32)[:, None], (blocks, pairs))
    x_pairs = jnp.repeat(tokens.reshape(blocks, TOK_SRC, D), TOPK, axis=1)
    cot_pairs = jnp.repeat(cotangent.reshape(blocks, TOK_SRC, D), TOPK, axis=1).astype(jnp.float32)
    dy_pairs = gates.reshape(blocks, pairs)[:, :, None] * cot_pairs
    x_buffer = jnp.zeros((EXPERTS, blocks, CAP, D), jnp.bfloat16).at[block_ids, block_index, slot].set(x_pairs)
    dy_buffer = jnp.zeros((EXPERTS, blocks, CAP, D), jnp.float32).at[block_ids, block_index, slot].set(dy_pairs)
    results = lax.map(expert_pass, (x_buffer.reshape(EXPERTS, blocks * CAP, D),
                                    dy_buffer.reshape(EXPERTS, blocks * CAP, D), w_gate, w_up, w_down))
    y_all, dx_all, grad_gate, grad_up, grad_down = results
    y_all = y_all.reshape(EXPERTS, blocks, CAP, D)
    dx_all = dx_all.reshape(EXPERTS, blocks, CAP, D)
    y_pairs = y_all[block_ids, block_index, slot].astype(jnp.float32).reshape(TOKENS, TOPK, D)
    dx_pairs = dx_all[block_ids, block_index, slot].astype(jnp.float32).reshape(TOKENS, TOPK, D)
    mixed = jnp.sum(gates[:, :, None] * y_pairs, axis=1).astype(jnp.bfloat16)
    d_tokens = jnp.sum(dx_pairs, axis=1).astype(jnp.bfloat16)
    d_gates = jnp.sum(cotangent.astype(jnp.float32)[:, None, :] * y_pairs, axis=2)
    return mixed, d_tokens, d_gates, grad_gate, grad_up, grad_down
```

```python
import jax
import jax.numpy as jnp
from jax import lax
from jax.sharding import PartitionSpec as P

TOPK = 4
EXP_GROUP = 4
PLANE = ("expert", "row")
F32 = jnp.float32
BF16 = jnp.bfloat16


def narrowed(value):
    return lax.reduce_precision(value, 8, 7)


def in_parts(value, count):
    parts = []
    for _ in range(count):
        top = narrowed(value)
        parts.append(top.astype(BF16))
        value = value - top
    return parts


def told_to_all(value, axis):
    peers = lax.axis_size(axis)
    return lax.all_to_all(
        jnp.broadcast_to(value[None], (peers, *value.shape)), axis, 0, 0, tiled=True
    )


def dispatched(tokens, cotangent, expert_ids, gates):
    width = tokens.shape[1]
    own = jnp.concatenate(
        [tokens, cotangent, expert_ids.astype(BF16), *in_parts(gates, 3)], axis=1
    )
    every = told_to_all(own, PLANE)
    every = every.reshape(-1, own.shape[1])
    ids = every[:, 2 * width : 2 * width + TOPK].astype(jnp.int32)
    parts = every[:, 2 * width + TOPK :].astype(F32)
    weights = parts[:, :TOPK] + parts[:, TOPK : 2 * TOPK] + parts[:, 2 * TOPK :]
    return every[:, :width], every[:, width : 2 * width], ids, weights


def routed(rows, tok_all, cot_all, match, gate_of, place, w_gate, w_up, w_down):
    chunks = lax.axis_size("col")
    chunk = rows // chunks
    ff = w_gate.shape[2]
    row_ids = jnp.arange(rows, dtype=jnp.int32)
    picks = jnp.stack([(place[:, e][None, :] == row_ids[:, None]) for e in range(EXP_GROUP)])
    pick_bf = picks.astype(BF16)
    both = jnp.concatenate([tok_all, cot_all], axis=1)
    spread = jnp.einsum("ert,td->erd", pick_bf, both, preferred_element_type=F32).astype(BF16)
    width = tok_all.shape[1]
    x_rows, c_rows = spread[:, :, :width], spread[:, :, width:]
    gate_part = jnp.einsum("erd,edf->rf", x_rows, w_gate, preferred_element_type=F32)
    up_part = jnp.einsum("erd,edf->rf", x_rows, w_up, preferred_element_type=F32)
    dh_part = jnp.einsum("erd,efd->rf", c_rows, w_down, preferred_element_type=F32)
    parts = jnp.concatenate([gate_part, up_part, dh_part], axis=1).astype(BF16)
    pieces = lax.all_to_all(parts.reshape(chunks, chunk, 3 * ff), "col", 0, 0, tiled=True)
    sums = jnp.sum(pieces.astype(F32), axis=0)
    gate_pre, up_pre, dh_raw = sums[:, :ff], sums[:, ff : 2 * ff], sums[:, 2 * ff :]
    mine = lax.axis_index("col") * chunk + jnp.arange(chunk, dtype=jnp.int32)
    row_gate = sum(
        jnp.sum(
            jnp.where(place[:, e][None, :] == mine[:, None], gate_of[:, e][None, :], 0.0),
            axis=1,
            keepdims=True,
        )
        for e in range(EXP_GROUP)
    )
    sigma = jax.nn.sigmoid(gate_pre)
    silu = gate_pre * sigma
    hidden = silu * up_pre
    dh = dh_raw * row_gate
    d_gate_pre = dh * up_pre * sigma * (1.0 + gate_pre * (1.0 - sigma))
    d_up_pre = dh * silu
    gate_term = jnp.sum(dh_raw * hidden, axis=1, keepdims=True)
    own = jnp.concatenate(
        [
            (hidden * row_gate).astype(BF16),
            d_gate_pre.astype(BF16),
            d_up_pre.astype(BF16),
            *in_parts(gate_term, 2),
        ],
        axis=1,
    )
    full = lax.all_gather(own, "col", axis=0, tiled=True)
    by_token = jnp.einsum("ert,rf->etf", pick_bf, full, preferred_element_type=F32).astype(BF16)
    hid, dgp, dup = by_token[:, :, :ff], by_token[:, :, ff : 2 * ff], by_token[:, :, 2 * ff : 3 * ff]
    mixed_part = jnp.einsum("etf,efd->td", hid, w_down, preferred_element_type=F32)
    dtok_part = jnp.einsum("etf,ekf->tk", dgp, w_gate, preferred_element_type=F32) + jnp.einsum(
        "etf,ekf->tk", dup, w_up, preferred_element_type=F32
    )
    term = by_token[:, :, 3 * ff].astype(F32) + by_token[:, :, 3 * ff + 1].astype(F32)
    term_k = jnp.sum(jnp.where(match, term.T[:, None, :], 0.0), axis=2)
    send = jnp.concatenate(
        [mixed_part.astype(BF16), dtok_part.astype(BF16), *in_parts(term_k, 2)], axis=1
    )
    peers = lax.axis_size(PLANE)
    back = lax.all_to_all(send.reshape(peers, -1, send.shape[1]), PLANE, 0, 0, tiled=True)
    grad_gate = jnp.einsum("td,etf->edf", tok_all, dgp, preferred_element_type=F32).astype(BF16)
    grad_up = jnp.einsum("td,etf->edf", tok_all, dup, preferred_element_type=F32).astype(BF16)
    grad_down = jnp.einsum("etf,td->efd", hid, cot_all, preferred_element_type=F32).astype(BF16)
    total = jnp.sum(back.astype(F32), axis=0)
    mixed = total[:, :width].astype(BF16)
    d_tokens = total[:, width : 2 * width].astype(BF16)
    d_gates = total[:, 2 * width : 2 * width + TOPK] + total[:, 2 * width + TOPK :]
    return mixed, d_tokens, d_gates, grad_gate, grad_up, grad_down


def local(tokens, cotangent, w_gate, w_up, w_down, expert_ids, gates):
    tok_all, cot_all, ids, weights = dispatched(tokens, cotangent, expert_ids, gates)
    count = ids.shape[0]
    here = ids - lax.axis_index("expert") * EXP_GROUP
    match = here[:, :, None] == jnp.arange(EXP_GROUP, dtype=jnp.int32)[None, None, :]
    used = jnp.any(match, axis=1)
    gate_of = jnp.sum(jnp.where(match, weights[:, :, None], 0.0), axis=1)
    order = jnp.arange(count, dtype=jnp.int32)
    before = (order[None, :] < order[:, None]).astype(BF16)
    ahead = jnp.sum(
        jnp.dot(before, used.astype(BF16), preferred_element_type=F32), axis=1, keepdims=True
    ).astype(jnp.int32)
    inner = jnp.cumsum(used.astype(jnp.int32), axis=1) - used.astype(jnp.int32)
    place = jnp.where(used, ahead + inner, -1)
    return routed(1024, tok_all, cot_all, match, gate_of, place, w_gate, w_up, w_down)


def solution(mesh):
    in_specs = (
        P(("expert", "row"), "col"),
        P(("expert", "row"), "col"),
        P("expert", "col", "row"),
        P("expert", "col", "row"),
        P("expert", "row", "col"),
        P(("expert", "row"), None),
        P(("expert", "row"), None),
    )
    out_specs = (
        P(("expert", "row"), "col"),
        P(("expert", "row"), "col"),
        P(("expert", "row"), None),
        P("expert", "col", "row"),
        P("expert", "col", "row"),
        P("expert", "row", "col"),
    )
    return jax.shard_map(local, mesh=mesh, in_specs=in_specs, out_specs=out_specs, check_vma=False)
```

```python
import jax
import jax.numpy as jnp
from jax import lax
from jax.sharding import PartitionSpec as P

TOPK = 4
EXP_GROUP = 4
PLANE = ("expert", "row")
F32 = jnp.float32
BF16 = jnp.bfloat16


def narrowed(value):
    return lax.reduce_precision(value, 8, 7)


def in_parts(value, count):
    parts = []
    for _ in range(count):
        top = narrowed(value)
        parts.append(top.astype(BF16))
        value = value - top
    return parts


def told_to_all(value, axis):
    peers = lax.axis_size(axis)
    return lax.all_to_all(
        jnp.broadcast_to(value[None], (peers, *value.shape)), axis, 0, 0, tiled=True
    )


def swapped(value):
    pairs = [(i, i ^ 8) for i in range(lax.axis_size(PLANE))]
    return lax.ppermute(value, PLANE, pairs)


def same_core():
    rows = lax.axis_size("row")
    groups = lax.axis_size("expert")
    return [
        [e * rows + r for e in range(core, groups, 2) for r in range(rows)] for core in range(2)
    ]


def over_chips(value):
    return lax.all_to_all(value, PLANE, 0, 0, axis_index_groups=same_core(), tiled=True)


def dispatched(tokens, cotangent, expert_ids, gates, second):
    width = tokens.shape[1]
    meta = jnp.concatenate([expert_ids.astype(BF16), *in_parts(gates, 3)], axis=1)
    first_kind = jnp.concatenate([tokens, meta], axis=1)
    other_kind = jnp.concatenate([cotangent, meta], axis=1)
    keep = jnp.where(second, other_kind, first_kind)
    got = swapped(jnp.where(second, first_kind, other_kind))
    pair = jnp.where(second, jnp.stack([got, keep]), jnp.stack([keep, got]))
    chips = lax.axis_size(PLANE) // 2
    every = over_chips(jnp.broadcast_to(pair[None], (chips, *pair.shape)))
    every = every.reshape(-1, every.shape[-1])
    across = swapped(every)
    ids = every[:, width : width + TOPK].astype(jnp.int32)
    parts = every[:, width + TOPK :].astype(F32)
    weights = parts[:, :TOPK] + parts[:, TOPK : 2 * TOPK] + parts[:, 2 * TOPK :]
    tok_all = jnp.where(second, across, every)[:, :width]
    cot_all = jnp.where(second, every, across)[:, :width]
    return tok_all, cot_all, ids, weights


def by_rows(rows, tok_all, cot_all, gate_of, place, w_gate, w_up, w_down):
    chunks = lax.axis_size("col")
    chunk = rows // chunks
    ff = w_gate.shape[2]
    row_ids = jnp.arange(rows, dtype=jnp.int32)
    picks = jnp.stack([(place[:, e][None, :] == row_ids[:, None]) for e in range(EXP_GROUP)])
    pick_bf = picks.astype(BF16)
    both = jnp.concatenate([tok_all, cot_all], axis=1)
    spread = jnp.einsum("ert,td->erd", pick_bf, both, preferred_element_type=F32).astype(BF16)
    width = tok_all.shape[1]
    x_rows, c_rows = spread[:, :, :width], spread[:, :, width:]
    gate_part = jnp.einsum("erd,edf->rf", x_rows, w_gate, preferred_element_type=F32)
    up_part = jnp.einsum("erd,edf->rf", x_rows, w_up, preferred_element_type=F32)
    dh_part = jnp.einsum("erd,efd->rf", c_rows, w_down, preferred_element_type=F32)
    parts = jnp.concatenate([gate_part, up_part, dh_part], axis=1).astype(BF16)
    pieces = lax.all_to_all(parts.reshape(chunks, chunk, 3 * ff), "col", 0, 0, tiled=True)
    sums = jnp.sum(pieces.astype(F32), axis=0)
    gate_pre, up_pre, dh_raw = sums[:, :ff], sums[:, ff : 2 * ff], sums[:, 2 * ff :]
    mine = lax.axis_index("col") * chunk + jnp.arange(chunk, dtype=jnp.int32)
    row_gate = sum(
        jnp.sum(
            jnp.where(place[:, e][None, :] == mine[:, None], gate_of[:, e][None, :], 0.0),
            axis=1,
            keepdims=True,
        )
        for e in range(EXP_GROUP)
    )
    sigma = jax.nn.sigmoid(gate_pre)
    silu = gate_pre * sigma
    hidden = silu * up_pre
    dh = dh_raw * row_gate
    d_gate_pre = dh * up_pre * sigma * (1.0 + gate_pre * (1.0 - sigma))
    d_up_pre = dh * silu
    gate_term = jnp.sum(dh_raw * hidden, axis=1, keepdims=True)
    own = jnp.concatenate(
        [
            (hidden * row_gate).astype(BF16),
            d_gate_pre.astype(BF16),
            d_up_pre.astype(BF16),
            *in_parts(gate_term, 2),
        ],
        axis=1,
    )
    full = told_to_all(own, "col").reshape(rows, own.shape[1])
    return jnp.einsum("ert,rf->etf", pick_bf, full, preferred_element_type=F32).astype(BF16)


SIZES = (704, 1024)


def local(tokens, cotangent, w_gate, w_up, w_down, expert_ids, gates):
    second = lax.axis_index("expert") % 2 == 1
    width = tokens.shape[1]
    ff = w_gate.shape[2]
    tok_all, cot_all, ids, weights = dispatched(tokens, cotangent, expert_ids, gates, second)
    count = ids.shape[0]
    here = ids - lax.axis_index("expert") * EXP_GROUP
    match = here[:, :, None] == jnp.arange(EXP_GROUP, dtype=jnp.int32)[None, None, :]
    used = jnp.any(match, axis=1)
    gate_of = jnp.sum(jnp.where(match, weights[:, :, None], 0.0), axis=1)
    order = jnp.arange(count, dtype=jnp.int32)
    before = (order[None, :] < order[:, None]).astype(BF16)
    ahead = jnp.sum(
        jnp.dot(before, used.astype(BF16), preferred_element_type=F32), axis=1, keepdims=True
    ).astype(jnp.int32)
    inner = jnp.cumsum(used.astype(jnp.int32), axis=1) - used.astype(jnp.int32)
    place = jnp.where(used, ahead + inner, -1)
    group_ids = jnp.arange(lax.axis_size("expert"), dtype=jnp.int32)
    fullest = jnp.max(
        jnp.sum((ids[:, :, None] // EXP_GROUP == group_ids).astype(jnp.int32), axis=(0, 1))
    )
    level = sum((fullest > size).astype(jnp.int32) for size in SIZES[:-1])
    by_token = lax.switch(
        level,
        [lambda *a, size=size: by_rows(size, *a) for size in SIZES],
        tok_all,
        cot_all,
        gate_of,
        place,
        w_gate,
        w_up,
        w_down,
    )
    hid, dgp, dup = by_token[:, :, :ff], by_token[:, :, ff : 2 * ff], by_token[:, :, 2 * ff : 3 * ff]
    mixed_part = jnp.einsum("etf,efd->td", hid, w_down, preferred_element_type=F32)
    dtok_part = jnp.einsum("etf,ekf->tk", dgp, w_gate, preferred_element_type=F32) + jnp.einsum(
        "etf,ekf->tk", dup, w_up, preferred_element_type=F32
    )
    term = by_token[:, :, 3 * ff].astype(F32) + by_token[:, :, 3 * ff + 1].astype(F32)
    term_k = jnp.sum(jnp.where(match, term.T[:, None, :], 0.0), axis=2)
    main = jnp.concatenate([mixed_part, dtok_part], axis=1)
    halves = jnp.concatenate([main.astype(BF16), *in_parts(term_k, 2)], axis=1)
    chips = lax.axis_size(PLANE) // 2
    halves = halves.reshape(chips, 2, -1, halves.shape[1])
    got = swapped(jnp.where(second, halves[:, 0], halves[:, 1])).astype(F32)
    keep = jnp.where(second, halves[:, 1], halves[:, 0]).astype(F32)
    joined = keep + got
    wide = 2 * width
    terms = joined[:, :, wide : wide + TOPK] + joined[:, :, wide + TOPK :]
    send = jnp.concatenate([joined[:, :, :wide].astype(BF16), *in_parts(terms, 2)], axis=2)
    back = over_chips(send)
    grad_gate = jnp.einsum("td,etf->edf", tok_all, dgp, preferred_element_type=F32).astype(BF16)
    grad_up = jnp.einsum("td,etf->edf", tok_all, dup, preferred_element_type=F32).astype(BF16)
    grad_down = jnp.einsum("etf,td->efd", hid, cot_all, preferred_element_type=F32).astype(BF16)
    total = jnp.sum(back.astype(F32), axis=0)
    mixed = total[:, :width].astype(BF16)
    d_tokens = total[:, width:wide].astype(BF16)
    d_gates = total[:, wide : wide + TOPK] + total[:, wide + TOPK :]
    return mixed, d_tokens, d_gates, grad_gate, grad_up, grad_down


def solution(mesh):
    in_specs = (
        P(("expert", "row"), "col"),
        P(("expert", "row"), "col"),
        P("expert", "col", "row"),
        P("expert", "col", "row"),
        P("expert", "row", "col"),
        P(("expert", "row"), None),
        P(("expert", "row"), None),
    )
    out_specs = (
        P(("expert", "row"), "col"),
        P(("expert", "row"), "col"),
        P(("expert", "row"), None),
        P("expert", "col", "row"),
        P("expert", "col", "row"),
        P("expert", "row", "col"),
    )
    return jax.shard_map(local, mesh=mesh, in_specs=in_specs, out_specs=out_specs, check_vma=False)
```

```python
import jax
import jax.numpy as jnp
from jax import lax
from jax.experimental import pallas as pl
from jax.experimental.pallas import tpu as pltpu
from jax.sharding import PartitionSpec as P

TOPK = 4
EXP_GROUP = 4
PLANE = ("expert", "row")
F32 = jnp.float32
BF16 = jnp.bfloat16


def narrowed(value):
    return lax.reduce_precision(value, 8, 7)


def in_parts(value, count):
    parts = []
    for _ in range(count):
        top = narrowed(value)
        parts.append(top.astype(BF16))
        value = value - top
    return parts


def told_to_all(value, axis):
    peers = lax.axis_size(axis)
    return lax.all_to_all(
        jnp.broadcast_to(value[None], (peers, *value.shape)), axis, 0, 0, tiled=True
    )


def swapped(value):
    pairs = [(i, i ^ 8) for i in range(lax.axis_size(PLANE))]
    return lax.ppermute(value, PLANE, pairs)


def same_core():
    rows = lax.axis_size("row")
    groups = lax.axis_size("expert")
    return [
        [e * rows + r for e in range(core, groups, 2) for r in range(rows)] for core in range(2)
    ]


def over_chips(value):
    return lax.all_to_all(value, PLANE, 0, 0, axis_index_groups=same_core(), tiled=True)


def dispatched(tokens, cotangent, expert_ids, gates, second):
    width = tokens.shape[1]
    meta = jnp.concatenate([expert_ids.astype(BF16), *in_parts(gates, 3)], axis=1)
    first_kind = jnp.concatenate([tokens, meta], axis=1)
    other_kind = jnp.concatenate([cotangent, meta], axis=1)
    keep = jnp.where(second, other_kind, first_kind)
    got = swapped(jnp.where(second, first_kind, other_kind))
    pair = jnp.where(second, jnp.stack([got, keep]), jnp.stack([keep, got]))
    chips = lax.axis_size(PLANE) // 2
    every = over_chips(jnp.broadcast_to(pair[None], (chips, *pair.shape)))
    every = every.reshape(-1, every.shape[-1])
    across = swapped(every)
    ids = every[:, width : width + TOPK].astype(jnp.int32)
    parts = every[:, width + TOPK :].astype(F32)
    weights = parts[:, :TOPK] + parts[:, TOPK : 2 * TOPK] + parts[:, 2 * TOPK :]
    return every, across, ids, weights


SIZES = (576, 640, 704, 1024)
SLAB = 272
PIECE = 384
VMEM = pl.BlockSpec(memory_space=pltpu.VMEM)
SMEM = pl.BlockSpec(memory_space=pltpu.SMEM)
NT = (((1,), (1,)), ((), ()))
TN = (((0,), (0,)), ((), ()))


def mult(a, b, dims=(((1,), (0,)), ((), ()))):
    return lax.dot_general(a, b, dims, preferred_element_type=F32)


def parts_kernel(info, every, across, place_t, w_gate, w_up, w_down, out, x_out, c_out, acc):
    depth = w_gate.shape[1]
    count = every.shape[0]
    acc[...] = jnp.zeros_like(acc)
    second = info[4] == 1

    def step(e, carry):
        start = pl.multiple_of(info[e], 16)
        where = place_t[pl.ds(e, 1), :] - start
        rows = lax.broadcasted_iota(jnp.int32, (SLAB, count), 0)
        pick = (rows == where).astype(F32).astype(BF16)
        one = mult(pick, every[...]).astype(BF16)
        two = mult(pick, across[...]).astype(BF16)
        x = jnp.where(second, two, one)[:, :depth]
        c = jnp.where(second, one, two)[:, :depth]
        x_out[e] = x
        c_out[e] = c
        span = pl.ds(start, SLAB)
        wide = w_gate.shape[2]
        acc[span, 0:wide] += mult(x, w_gate[e])
        acc[span, PIECE : PIECE + wide] += mult(x, w_up[e])
        acc[span, 2 * PIECE : 2 * PIECE + wide] += mult(c, w_down[e], NT)
        return carry

    lax.fori_loop(0, EXP_GROUP, step, 0)
    out[...] = acc[...].astype(BF16)


def middle_kernel(info, pieces, place_t, gate_t, out):
    chunk = pieces.shape[1]
    count = place_t.shape[1]
    total = pieces[0].astype(F32)
    for p in range(1, pieces.shape[0]):
        total = total + pieces[p].astype(F32)
    gate_pre = total[:, :PIECE]
    up_pre = total[:, PIECE : 2 * PIECE]
    dh_raw = total[:, 2 * PIECE :]
    rows = lax.broadcasted_iota(jnp.int32, (chunk, count), 0) + info[5] * chunk
    found = jnp.zeros((chunk, count), F32)
    for e in range(EXP_GROUP):
        found = found + jnp.where(rows == place_t[e : e + 1, :], gate_t[e : e + 1, :], 0.0)
    row_gate = jnp.sum(found, axis=1, keepdims=True)
    sigma = jax.nn.sigmoid(gate_pre)
    silu = gate_pre * sigma
    hidden = silu * up_pre
    dh = dh_raw * row_gate
    d_gate_pre = dh * up_pre * sigma * (1.0 + gate_pre * (1.0 - sigma))
    d_up_pre = dh * silu
    term = jnp.sum(dh_raw * hidden, axis=1, keepdims=True)
    top = term.astype(BF16).astype(F32)
    lanes = lax.broadcasted_iota(jnp.int32, (chunk, PIECE), 1)
    scaled = hidden * row_gate
    scaled = jnp.where(lanes == PIECE - 24, top, scaled)
    scaled = jnp.where(lanes == PIECE - 23, term - top, scaled)
    own = jnp.concatenate([scaled, d_gate_pre, d_up_pre], axis=1).astype(BF16)
    for p in range(out.shape[0]):
        out[p] = own


def tokens_kernel(info, full, place, here, w_gate, w_up, w_down, keep, send, acc):
    count = place.shape[0]
    ff = w_gate.shape[2]
    width = w_gate.shape[1]
    acc[...] = jnp.zeros_like(acc)
    lane = lax.broadcasted_iota(jnp.int32, place.shape, 1)

    def step(e, carry):
        start = pl.multiple_of(info[e], 16)
        where = jnp.sum(jnp.where(lane == e, place[...], 0), axis=1, keepdims=True) - start
        cols = lax.broadcasted_iota(jnp.int32, (count, SLAB), 1)
        pick = (cols == where).astype(F32).astype(BF16)
        got = mult(pick, full[pl.ds(start, SLAB), :])
        hid = got[:, :PIECE]
        at = lax.broadcasted_iota(jnp.int32, hid.shape, 1)
        term = jnp.sum(jnp.where(at >= ff, hid, 0.0), axis=1, keepdims=True)
        got = got.astype(BF16)
        acc[:, 0:width] += mult(got[:, :ff], w_down[e])
        acc[:, PIECE : PIECE + width] += mult(
            got[:, PIECE : PIECE + ff], w_gate[e], NT
        ) + mult(got[:, 2 * PIECE : 2 * PIECE + ff], w_up[e], NT)
        acc[:, 2 * PIECE : 2 * PIECE + TOPK] += jnp.where(here[...] == e, term, 0.0)
        return carry

    lax.fori_loop(0, EXP_GROUP, step, 0)
    term = acc[:, 2 * PIECE : 2 * PIECE + TOPK]
    top = term.astype(BF16).astype(F32)
    acc[:, PIECE - 24 : PIECE - 24 + TOPK] = top
    acc[:, PIECE - 16 : PIECE - 16 + TOPK] = term - top
    block = send.shape[1]
    mine = info[4]

    def copy(chip, carry):
        a = pl.multiple_of((2 * chip + mine) * block, block)
        b = pl.multiple_of((2 * chip + 1 - mine) * block, block)
        keep[chip] = acc[pl.ds(a, block), 0 : 2 * PIECE]
        send[chip] = acc[pl.ds(b, block), 0 : 2 * PIECE].astype(BF16)
        return carry

    lax.fori_loop(0, send.shape[0], copy, 0)


def join_kernel(keep, got, out):
    total = keep[...] + got[...].astype(F32)
    head = total[:, :, :PIECE]
    term = head[:, :, PIECE - 24 : PIECE - 24 + TOPK] + head[:, :, PIECE - 16 : PIECE - 16 + TOPK]
    top = term.astype(BF16)
    out[...] = total.astype(BF16)
    out[:, :, PIECE - 24 : PIECE - 24 + TOPK] = top
    out[:, :, PIECE - 16 : PIECE - 16 + TOPK] = (term - top.astype(F32)).astype(BF16)


def last_kernel(back, mixed, d_tokens, d_gates):
    total = back[0].astype(F32)
    for p in range(1, back.shape[0]):
        total = total + back[p].astype(F32)
    width = mixed.shape[1]
    mixed[...] = total[:, :width].astype(BF16)
    d_tokens[...] = total[:, PIECE : PIECE + width].astype(BF16)
    d_gates[...] = (
        total[:, PIECE - 24 : PIECE - 24 + TOPK] + total[:, PIECE - 16 : PIECE - 16 + TOPK]
    )


def grads_kernel(info, full, x_rows, c_rows, g_gate, g_up, g_down):
    ff = g_gate.shape[2]

    def step(e, carry):
        start = pl.multiple_of(info[e], 16)
        slab = full[pl.ds(start, SLAB), :]
        x = x_rows[e]
        c = c_rows[e]
        g_gate[e] = mult(x, slab[:, PIECE : PIECE + ff], TN).astype(BF16)
        g_up[e] = mult(x, slab[:, 2 * PIECE : 2 * PIECE + ff], TN).astype(BF16)
        g_down[e] = mult(slab[:, :ff], c, TN).astype(BF16)
        return carry

    lax.fori_loop(0, EXP_GROUP, step, 0)


def called(kernel, outs, n_in, first=SMEM, scratch=()):
    one = not isinstance(outs, (list, tuple))
    return pl.pallas_call(
        kernel,
        out_shape=outs,
        in_specs=[first] + [VMEM] * (n_in - 1),
        out_specs=VMEM if one else [VMEM] * len(outs),
        scratch_shapes=list(scratch),
    )


def of(shape, dtype):
    return jax.ShapeDtypeStruct(shape, dtype)


def routed(rows, every, across, here, gate_of, rank, begin, w_gate, w_up, w_down):
    chunks = lax.axis_size("col")
    chunk = rows // chunks
    chips = lax.axis_size(PLANE) // 2
    tok = every.shape[0] // (2 * chips)
    depth, ff = w_gate.shape[1:]
    start = jnp.minimum(begin // 16 * 16, rows - SLAB)
    core = lax.axis_index("expert") % 2
    info = jnp.concatenate([start, jnp.stack([core, lax.axis_index("col")])]).astype(jnp.int32)
    place_t = rank.T
    parts, x_rows, c_rows = called(
        parts_kernel,
        [
            of((rows, 3 * PIECE), BF16),
            of((EXP_GROUP, SLAB, depth), BF16),
            of((EXP_GROUP, SLAB, depth), BF16),
        ],
        7,
        scratch=[pltpu.VMEM((rows, 3 * PIECE), F32)],
    )(info, every, across, place_t, w_gate, w_up, w_down)
    pieces = lax.all_to_all(parts.reshape(chunks, chunk, 3 * PIECE), "col", 0, 0, tiled=True)
    own = called(middle_kernel, of((chunks, chunk, 3 * PIECE), BF16), 4)(
        info, pieces, place_t, gate_of.T
    )
    full = lax.all_to_all(own, "col", 0, 0, tiled=True).reshape(rows, 3 * PIECE)
    keep, send = called(
        tokens_kernel,
        [of((chips, tok, 2 * PIECE), F32), of((chips, tok, 2 * PIECE), BF16)],
        7,
        scratch=[pltpu.VMEM((every.shape[0], 3 * PIECE), F32)],
    )(info, full, rank, here, w_gate, w_up, w_down)
    got = swapped(send)
    joined = called(join_kernel, of((chips, tok, 2 * PIECE), BF16), 2, first=VMEM)(keep, got)
    back = over_chips(joined)
    g_gate, g_up, g_down = called(
        grads_kernel,
        [of(w_gate.shape, BF16), of(w_up.shape, BF16), of(w_down.shape, BF16)],
        4,
    )(info, full, x_rows, c_rows)
    mixed, d_tokens, d_gates = called(
        last_kernel,
        [of((tok, depth), BF16), of((tok, depth), BF16), of((tok, TOPK), F32)],
        1,
        first=VMEM,
    )(back)
    return mixed, d_tokens, d_gates, g_gate, g_up, g_down


def local(tokens, cotangent, w_gate, w_up, w_down, expert_ids, gates):
    second = lax.axis_index("expert") % 2 == 1
    every, across, ids, weights = dispatched(tokens, cotangent, expert_ids, gates, second)
    count = ids.shape[0]
    here = ids - lax.axis_index("expert") * EXP_GROUP
    match = here[:, :, None] == jnp.arange(EXP_GROUP, dtype=jnp.int32)[None, None, :]
    used = jnp.any(match, axis=1)
    gate_of = jnp.sum(jnp.where(match, weights[:, :, None], 0.0), axis=1)
    order = jnp.arange(count, dtype=jnp.int32)
    before = (order[None, :] < order[:, None]).astype(BF16)
    ahead = jnp.dot(before, used.astype(BF16), preferred_element_type=F32).astype(jnp.int32)
    held = jnp.sum(used.astype(jnp.int32), axis=0)
    begin = jnp.cumsum(held) - held
    rank = jnp.where(used, ahead + begin[None, :], -(1 << 20))
    group_ids = jnp.arange(lax.axis_size("expert"), dtype=jnp.int32)
    fullest = jnp.max(
        jnp.sum((ids[:, :, None] // EXP_GROUP == group_ids).astype(jnp.int32), axis=(0, 1))
    )
    level = sum((fullest > size).astype(jnp.int32) for size in SIZES[:-1])
    return lax.switch(
        level,
        [lambda *a, size=size: routed(size, *a) for size in SIZES],
        every,
        across,
        here,
        gate_of,
        rank,
        begin,
        w_gate,
        w_up,
        w_down,
    )


def solution(mesh):
    in_specs = (
        P(("expert", "row"), "col"),
        P(("expert", "row"), "col"),
        P("expert", "col", "row"),
        P("expert", "col", "row"),
        P("expert", "row", "col"),
        P(("expert", "row"), None),
        P(("expert", "row"), None),
    )
    out_specs = (
        P(("expert", "row"), "col"),
        P(("expert", "row"), "col"),
        P(("expert", "row"), None),
        P("expert", "col", "row"),
        P("expert", "col", "row"),
        P("expert", "row", "col"),
    )
    return jax.shard_map(local, mesh=mesh, in_specs=in_specs, out_specs=out_specs, check_vma=False)
```

```python
import jax
import jax.numpy as jnp
from jax import lax
from jax.experimental import pallas as pl
from jax.experimental.pallas import tpu as pltpu
from jax.sharding import PartitionSpec as P

TOPK = 4
EXP_GROUP = 4
PLANE = ("expert", "row")
F32 = jnp.float32
BF16 = jnp.bfloat16


def swapped(value):
    pairs = [(i, i ^ 8) for i in range(lax.axis_size(PLANE))]
    return lax.ppermute(value, PLANE, pairs)


def same_core():
    rows = lax.axis_size("row")
    groups = lax.axis_size("expert")
    return [
        [e * rows + r for e in range(core, groups, 2) for r in range(rows)] for core in range(2)
    ]


def over_chips(value):
    return lax.all_to_all(value, PLANE, 0, 0, axis_index_groups=same_core(), tiled=True)


def dispatched(tokens, cotangent, expert_ids, gates, core):
    tok = tokens.shape[0]
    keep, send = called(
        pack_kernel, [of((tok, PIECE), BF16), of((tok, PIECE), BF16)], 5
    )(core, tokens, cotangent, expert_ids.T, gates.T)
    got = swapped(send)
    second = core[0] == 1
    pair = jnp.stack([jnp.where(second, got, keep), jnp.where(second, keep, got)])
    chips = lax.axis_size(PLANE) // 2
    every = over_chips(jnp.broadcast_to(pair[None], (chips, *pair.shape)))
    every = every.reshape(-1, PIECE)
    return every, swapped(every)


SIZES = (576, 640, 704, 1024)
SLAB = 272
PIECE = 384
VMEM = pl.BlockSpec(memory_space=pltpu.VMEM)
SMEM = pl.BlockSpec(memory_space=pltpu.SMEM)
NT = (((1,), (1,)), ((), ()))
TN = (((0,), (0,)), ((), ()))


def mult(a, b, dims=(((1,), (0,)), ((), ()))):
    return lax.dot_general(a, b, dims, preferred_element_type=F32)


def moved(value, first, lanes):
    rows = value.shape[0]
    at = lax.broadcasted_iota(jnp.int32, (rows, lanes), 1)
    src = lax.broadcasted_iota(jnp.int32, (rows, lanes), 0)
    put = (at == src + first).astype(F32).astype(BF16)
    return mult(value.astype(BF16), put, TN)


def pack_kernel(core, tokens, cotangent, ids_t, gates_t, keep, send):
    width = tokens.shape[1]
    rest = gates_t[...]
    meta = moved(ids_t[...].astype(F32), width, PIECE)
    for part in range(1, 4):
        top = rest.astype(BF16).astype(F32)
        meta = meta + moved(top, width + part * TOPK, PIECE)
        rest = rest - top
    second = core[0] == 1
    one = tokens[...].astype(F32)
    two = cotangent[...].astype(F32)
    keep[...] = meta.astype(BF16)
    send[...] = meta.astype(BF16)
    keep[:, :width] = jnp.where(second, two, one).astype(BF16)
    send[:, :width] = jnp.where(second, one, two).astype(BF16)


def route_kernel(core, every, place, place_t, gate_t, nums):
    count = every.shape[0]
    first = PIECE - 24
    groups = nums.shape[0] - EXP_GROUP
    group = core[1]
    at = lax.broadcasted_iota(jnp.int32, (16, PIECE), 1)
    row = lax.broadcasted_iota(jnp.int32, (16, PIECE), 0)
    meta = mult((at == row + first).astype(F32).astype(BF16), every[...], NT)
    ids = meta[0:TOPK]
    weights = meta[TOPK : 2 * TOPK] + meta[2 * TOPK : 3 * TOPK] + meta[3 * TOPK : 4 * TOPK]
    local_ids = ids - (group * EXP_GROUP).astype(F32)
    sub = lax.broadcasted_iota(jnp.int32, (8, count), 0)
    used = jnp.zeros((8, count), F32)
    gate = jnp.zeros((8, count), F32)
    for e in range(EXP_GROUP):
        hit = local_ids == float(e)
        any_hit = jnp.sum(jnp.where(hit, 1.0, 0.0), axis=0, keepdims=True)
        any_gate = jnp.sum(jnp.where(hit, weights, 0.0), axis=0, keepdims=True)
        used = jnp.where(sub == e, any_hit, used)
        gate = jnp.where(sub == e, any_gate, gate)
    gate_t[...] = gate
    a = lax.broadcasted_iota(jnp.int32, (count, count), 0)
    b = lax.broadcasted_iota(jnp.int32, (count, count), 1)
    ahead = mult(used.astype(BF16), (a < b).astype(F32).astype(BF16))
    begin = jnp.float32(0.0)
    for e in range(EXP_GROUP):
        nums[e] = begin.astype(jnp.int32)
        ahead = ahead + jnp.where(sub == e, begin, 0.0)
        begin = begin + jnp.sum(jnp.where(sub == e, used, 0.0))
    for g in range(groups):
        low = float(g * EXP_GROUP)
        inside = (ids >= low) & (ids < low + EXP_GROUP)
        nums[EXP_GROUP + g] = jnp.sum(jnp.where(inside, 1.0, 0.0)).astype(jnp.int32)
    spot = jnp.where(used > 0.0, ahead, -4096.0)
    place_t[...] = spot.astype(jnp.int32)
    high = jnp.floor(spot * (1.0 / 256.0))
    column = moved(high, 0, 128) * 256.0 + moved(spot - high * 256.0, 0, 128)
    place[...] = column.astype(jnp.int32)


def parts_kernel(info, every, across, place_t, w_gate, w_up, w_down, out, x_out, c_out, acc):
    depth = w_gate.shape[1]
    count = every.shape[0]
    acc[...] = jnp.zeros_like(acc)
    second = info[4] == 1

    def step(e, carry):
        start = pl.multiple_of(info[e], 16)
        where = place_t[pl.ds(e, 1), :] - start
        rows = lax.broadcasted_iota(jnp.int32, (SLAB, count), 0)
        pick = (rows == where).astype(F32).astype(BF16)
        one = mult(pick, every[...]).astype(BF16)
        two = mult(pick, across[...]).astype(BF16)
        x = jnp.where(second, two, one)[:, :depth]
        c = jnp.where(second, one, two)[:, :depth]
        x_out[e] = x
        c_out[e] = c
        span = pl.ds(start, SLAB)
        wide = w_gate.shape[2]
        acc[span, 0:wide] += mult(x, w_gate[e])
        acc[span, PIECE : PIECE + wide] += mult(x, w_up[e])
        acc[span, 2 * PIECE : 2 * PIECE + wide] += mult(c, w_down[e], NT)
        return carry

    lax.fori_loop(0, EXP_GROUP, step, 0)
    out[...] = acc[...].astype(BF16)


def middle_kernel(info, pieces, place_t, gate_t, out):
    chunk = pieces.shape[1]
    count = place_t.shape[1]
    total = pieces[0].astype(F32)
    for p in range(1, pieces.shape[0]):
        total = total + pieces[p].astype(F32)
    gate_pre = total[:, :PIECE]
    up_pre = total[:, PIECE : 2 * PIECE]
    dh_raw = total[:, 2 * PIECE :]
    rows = lax.broadcasted_iota(jnp.int32, (chunk, count), 0) + info[5] * chunk
    found = jnp.zeros((chunk, count), F32)
    for e in range(EXP_GROUP):
        found = found + jnp.where(rows == place_t[e : e + 1, :], gate_t[e : e + 1, :], 0.0)
    row_gate = jnp.sum(found, axis=1, keepdims=True)
    sigma = jax.nn.sigmoid(gate_pre)
    silu = gate_pre * sigma
    hidden = silu * up_pre
    dh = dh_raw * row_gate
    d_gate_pre = dh * up_pre * sigma * (1.0 + gate_pre * (1.0 - sigma))
    d_up_pre = dh * silu
    term = jnp.sum(dh_raw * hidden, axis=1, keepdims=True)
    top = term.astype(BF16).astype(F32)
    lanes = lax.broadcasted_iota(jnp.int32, (chunk, PIECE), 1)
    scaled = hidden * row_gate
    scaled = jnp.where(lanes == PIECE - 24, top, scaled)
    scaled = jnp.where(lanes == PIECE - 23, term - top, scaled)
    own = jnp.concatenate([scaled, d_gate_pre, d_up_pre], axis=1).astype(BF16)
    for p in range(out.shape[0]):
        out[p] = own


def tokens_kernel(info, full, place, every, w_gate, w_up, w_down, keep, send, acc):
    count = place.shape[0]
    ff = w_gate.shape[2]
    width = w_gate.shape[1]
    acc[...] = jnp.zeros_like(acc)
    lane = lax.broadcasted_iota(jnp.int32, place.shape, 1)
    here = every[:, PIECE - 128 :].astype(F32).astype(jnp.int32) - info[6] * EXP_GROUP

    def step(e, carry):
        start = pl.multiple_of(info[e], 16)
        where = jnp.sum(jnp.where(lane == e, place[...], 0), axis=1, keepdims=True) - start
        cols = lax.broadcasted_iota(jnp.int32, (count, SLAB), 1)
        pick = (cols == where).astype(F32).astype(BF16)
        got = mult(pick, full[pl.ds(start, SLAB), :])
        hid = got[:, :PIECE]
        at = lax.broadcasted_iota(jnp.int32, hid.shape, 1)
        term = jnp.sum(jnp.where(at >= ff, hid, 0.0), axis=1, keepdims=True)
        got = got.astype(BF16)
        acc[:, 0:width] += mult(got[:, :ff], w_down[e])
        acc[:, PIECE : PIECE + width] += mult(
            got[:, PIECE : PIECE + ff], w_gate[e], NT
        ) + mult(got[:, 2 * PIECE : 2 * PIECE + ff], w_up[e], NT)
        acc[:, 2 * PIECE : 2 * PIECE + 128] += jnp.where(here == e, term, 0.0)
        return carry

    lax.fori_loop(0, EXP_GROUP, step, 0)
    term = acc[:, 2 * PIECE + 104 : 2 * PIECE + 104 + TOPK]
    top = term.astype(BF16).astype(F32)
    acc[:, PIECE - 24 : PIECE - 24 + TOPK] = top
    acc[:, PIECE - 16 : PIECE - 16 + TOPK] = term - top
    block = send.shape[1]
    mine = info[4]

    def copy(chip, carry):
        a = pl.multiple_of((2 * chip + mine) * block, block)
        b = pl.multiple_of((2 * chip + 1 - mine) * block, block)
        keep[chip] = acc[pl.ds(a, block), 0 : 2 * PIECE]
        send[chip] = acc[pl.ds(b, block), 0 : 2 * PIECE].astype(BF16)
        return carry

    lax.fori_loop(0, send.shape[0], copy, 0)


def join_kernel(keep, got, out):
    total = keep[...] + got[...].astype(F32)
    head = total[:, :, :PIECE]
    term = head[:, :, PIECE - 24 : PIECE - 24 + TOPK] + head[:, :, PIECE - 16 : PIECE - 16 + TOPK]
    top = term.astype(BF16)
    out[...] = total.astype(BF16)
    out[:, :, PIECE - 24 : PIECE - 24 + TOPK] = top
    out[:, :, PIECE - 16 : PIECE - 16 + TOPK] = (term - top.astype(F32)).astype(BF16)


def last_kernel(back, mixed, d_tokens, d_gates):
    total = back[0].astype(F32)
    for p in range(1, back.shape[0]):
        total = total + back[p].astype(F32)
    width = mixed.shape[1]
    mixed[...] = total[:, :width].astype(BF16)
    d_tokens[...] = total[:, PIECE : PIECE + width].astype(BF16)
    d_gates[...] = (
        total[:, PIECE - 24 : PIECE - 24 + TOPK] + total[:, PIECE - 16 : PIECE - 16 + TOPK]
    )


def grads_kernel(info, full, x_rows, c_rows, g_gate, g_up, g_down):
    ff = g_gate.shape[2]

    def step(e, carry):
        start = pl.multiple_of(info[e], 16)
        slab = full[pl.ds(start, SLAB), :]
        x = x_rows[e]
        c = c_rows[e]
        g_gate[e] = mult(x, slab[:, PIECE : PIECE + ff], TN).astype(BF16)
        g_up[e] = mult(x, slab[:, 2 * PIECE : 2 * PIECE + ff], TN).astype(BF16)
        g_down[e] = mult(slab[:, :ff], c, TN).astype(BF16)
        return carry

    lax.fori_loop(0, EXP_GROUP, step, 0)


def called(kernel, outs, n_in, first=SMEM, scratch=()):
    one = not isinstance(outs, (list, tuple))
    return pl.pallas_call(
        kernel,
        out_shape=outs,
        in_specs=[first] + [VMEM] * (n_in - 1),
        out_specs=VMEM if one else [VMEM] * len(outs),
        scratch_shapes=list(scratch),
    )


def of(shape, dtype):
    return jax.ShapeDtypeStruct(shape, dtype)


def routed(rows, every, across, place, place_t, gate_t, begin, w_gate, w_up, w_down):
    chunks = lax.axis_size("col")
    chunk = rows // chunks
    chips = lax.axis_size(PLANE) // 2
    tok = every.shape[0] // (2 * chips)
    depth, ff = w_gate.shape[1:]
    start = jnp.minimum(begin // 16 * 16, rows - SLAB)
    group = lax.axis_index("expert")
    info = jnp.concatenate([start, jnp.stack([group % 2, lax.axis_index("col"), group])])
    parts, x_rows, c_rows = called(
        parts_kernel,
        [
            of((rows, 3 * PIECE), BF16),
            of((EXP_GROUP, SLAB, depth), BF16),
            of((EXP_GROUP, SLAB, depth), BF16),
        ],
        7,
        scratch=[pltpu.VMEM((rows, 3 * PIECE), F32)],
    )(info, every, across, place_t, w_gate, w_up, w_down)
    pieces = lax.all_to_all(parts.reshape(chunks, chunk, 3 * PIECE), "col", 0, 0, tiled=True)
    own = called(middle_kernel, of((chunks, chunk, 3 * PIECE), BF16), 4)(
        info, pieces, place_t, gate_t
    )
    full = lax.all_to_all(own, "col", 0, 0, tiled=True).reshape(rows, 3 * PIECE)
    keep, send = called(
        tokens_kernel,
        [of((chips, tok, 2 * PIECE), F32), of((chips, tok, 2 * PIECE), BF16)],
        7,
        scratch=[pltpu.VMEM((every.shape[0], 3 * PIECE), F32)],
    )(info, full, place, every, w_gate, w_up, w_down)
    got = swapped(send)
    joined = called(join_kernel, of((chips, tok, 2 * PIECE), BF16), 2, first=VMEM)(keep, got)
    back = over_chips(joined)
    g_gate, g_up, g_down = called(
        grads_kernel,
        [of(w_gate.shape, BF16), of(w_up.shape, BF16), of(w_down.shape, BF16)],
        4,
    )(info, full, x_rows, c_rows)
    mixed, d_tokens, d_gates = called(
        last_kernel,
        [of((tok, depth), BF16), of((tok, depth), BF16), of((tok, TOPK), F32)],
        1,
        first=VMEM,
    )(back)
    return mixed, d_tokens, d_gates, g_gate, g_up, g_down


def local(tokens, cotangent, w_gate, w_up, w_down, expert_ids, gates):
    group = lax.axis_index("expert")
    core = jnp.stack([group % 2, group]).astype(jnp.int32)
    every, across = dispatched(tokens, cotangent, expert_ids, gates, core)
    count = every.shape[0]
    groups = lax.axis_size("expert")
    place, place_t, gate_t, nums = pl.pallas_call(
        route_kernel,
        out_shape=[
            of((count, 128), jnp.int32),
            of((8, count), jnp.int32),
            of((8, count), F32),
            of((EXP_GROUP + groups,), jnp.int32),
        ],
        in_specs=[SMEM, VMEM],
        out_specs=[VMEM, VMEM, VMEM, SMEM],
    )(core, every)
    fullest = jnp.max(nums[EXP_GROUP:])
    level = sum((fullest > size).astype(jnp.int32) for size in SIZES[:-1])
    return lax.switch(
        level,
        [lambda *a, size=size: routed(size, *a) for size in SIZES],
        every,
        across,
        place,
        place_t,
        gate_t,
        nums[:EXP_GROUP],
        w_gate,
        w_up,
        w_down,
    )


def solution(mesh):
    in_specs = (
        P(("expert", "row"), "col"),
        P(("expert", "row"), "col"),
        P("expert", "col", "row"),
        P("expert", "col", "row"),
        P("expert", "row", "col"),
        P(("expert", "row"), None),
        P(("expert", "row"), None),
    )
    out_specs = (
        P(("expert", "row"), "col"),
        P(("expert", "row"), "col"),
        P(("expert", "row"), None),
        P("expert", "col", "row"),
        P("expert", "col", "row"),
        P("expert", "row", "col"),
    )
    return jax.shard_map(local, mesh=mesh, in_specs=in_specs, out_specs=out_specs, check_vma=False)
```

```python
from functools import partial

import jax
import jax.numpy as jnp
from jax import lax
from jax.experimental import pallas as pl
from jax.experimental.pallas import tpu as pltpu
from jax.sharding import PartitionSpec as P

TOPK = 4
EXP_GROUP = 4
PLANE = ("expert", "row")
F32 = jnp.float32
BF16 = jnp.bfloat16


def swapped(value):
    pairs = [(i, i ^ 8) for i in range(lax.axis_size(PLANE))]
    return lax.ppermute(value, PLANE, pairs)


def same_core():
    rows = lax.axis_size("row")
    groups = lax.axis_size("expert")
    return [
        [e * rows + r for e in range(core, groups, 2) for r in range(rows)] for core in range(2)
    ]


def over_chips(value):
    return lax.all_to_all(value, PLANE, 0, 0, axis_index_groups=same_core(), tiled=True)


def dispatched(tokens, cotangent, expert_ids, gates):
    tok = tokens.shape[0]
    keep, send = called(
        pack_kernel, [of((tok, PIECE), BF16), of((tok, PIECE), BF16)], 4, first=VMEM
    )(tokens, cotangent, expert_ids.T, gates.T)
    got = swapped(send)
    second = lax.axis_index("expert") % 2 == 1
    pair = jnp.stack([jnp.where(second, got, keep), jnp.where(second, keep, got)])
    chips = lax.axis_size(PLANE) // 2
    every = over_chips(jnp.broadcast_to(pair[None], (chips, *pair.shape)))
    every = every.reshape(-1, PIECE)
    return every, swapped(every)


SIZES = (704, 768, 1024)
SLAB = 272
PIECE = 384
VMEM = pl.BlockSpec(memory_space=pltpu.VMEM)
SMEM = pl.BlockSpec(memory_space=pltpu.SMEM)
NT = (((1,), (1,)), ((), ()))
TN = (((0,), (0,)), ((), ()))


def slab_of(info, e, rows):
    return pl.multiple_of(jnp.minimum((info[e] >> 4) << 4, rows - SLAB), 16)


def mult(a, b, dims=(((1,), (0,)), ((), ()))):
    return lax.dot_general(a, b, dims, preferred_element_type=F32)


def moved(value, first, lanes):
    rows = value.shape[0]
    at = lax.broadcasted_iota(jnp.int32, (rows, lanes), 1)
    src = lax.broadcasted_iota(jnp.int32, (rows, lanes), 0)
    put = (at == src + first).astype(F32).astype(BF16)
    return mult(value.astype(BF16), put, TN)


def pack_kernel(tokens, cotangent, ids_t, gates_t, keep, send):
    width = tokens.shape[1]
    rest = gates_t[...]
    meta = moved(ids_t[...].astype(F32), width, PIECE)
    for part in range(1, 4):
        top = rest.astype(BF16).astype(F32)
        meta = meta + moved(top, width + part * TOPK, PIECE)
        rest = rest - top
    second = lax.axis_index("expert") % 2 == 1
    one = tokens[...].astype(F32)
    two = cotangent[...].astype(F32)
    keep[...] = meta.astype(BF16)
    send[...] = meta.astype(BF16)
    keep[:, :width] = jnp.where(second, two, one).astype(BF16)
    send[:, :width] = jnp.where(second, one, two).astype(BF16)


def route_kernel(every, place, place_t, gate_t, info):
    count = every.shape[0]
    first = PIECE - 24
    groups = lax.axis_size("expert")
    group = lax.axis_index("expert")
    at = lax.broadcasted_iota(jnp.int32, (16, PIECE), 1)
    row = lax.broadcasted_iota(jnp.int32, (16, PIECE), 0)
    meta = mult((at == row + first).astype(F32).astype(BF16), every[...], NT)
    ids = meta[0:TOPK]
    weights = meta[TOPK : 2 * TOPK] + meta[2 * TOPK : 3 * TOPK] + meta[3 * TOPK : 4 * TOPK]
    local_ids = ids - (group * EXP_GROUP).astype(F32)
    sub = lax.broadcasted_iota(jnp.int32, (8, count), 0)
    used = jnp.zeros((8, count), F32)
    gate = jnp.zeros((8, count), F32)
    for e in range(EXP_GROUP):
        hit = local_ids == float(e)
        any_hit = jnp.sum(jnp.where(hit, 1.0, 0.0), axis=0, keepdims=True)
        any_gate = jnp.sum(jnp.where(hit, weights, 0.0), axis=0, keepdims=True)
        used = jnp.where(sub == e, any_hit, used)
        gate = jnp.where(sub == e, any_gate, gate)
    gate_t[...] = gate
    a = lax.broadcasted_iota(jnp.int32, (count, count), 0)
    b = lax.broadcasted_iota(jnp.int32, (count, count), 1)
    ahead = mult(used.astype(BF16), (a < b).astype(F32).astype(BF16))
    begin = jnp.float32(0.0)
    for e in range(EXP_GROUP):
        info[e] = begin.astype(jnp.int32)
        ahead = ahead + jnp.where(sub == e, begin, 0.0)
        begin = begin + jnp.sum(jnp.where(sub == e, used, 0.0))
    fullest = jnp.float32(0.0)
    for g in range(groups):
        low = float(g * EXP_GROUP)
        inside = (ids >= low) & (ids < low + EXP_GROUP)
        fullest = jnp.maximum(fullest, jnp.sum(jnp.where(inside, 1.0, 0.0)))
    level = jnp.int32(0)
    for size in SIZES[:-1]:
        level = level + (fullest > float(size)).astype(jnp.int32)
    info[4] = group % 2
    info[5] = lax.axis_index("col")
    info[6] = group
    info[7] = level
    spot = jnp.where(used > 0.0, ahead, -4096.0)
    place_t[...] = spot.astype(jnp.int32)
    high = jnp.floor(spot * (1.0 / 256.0))
    column = moved(high, 0, 128) * 256.0 + moved(spot - high * 256.0, 0, 128)
    place[...] = column.astype(jnp.int32)


def parts_kernel(turn, info, every, across, place_t, w_gate, w_up, w_down, x_out, c_out, *rest):
    outs, acc = rest[:-1], rest[-1]
    depth = w_gate.shape[1]
    count = every.shape[0]
    acc[...] = jnp.zeros_like(acc)
    second = info[4] == 1

    def step(e, carry):
        start = slab_of(info, e, acc.shape[0])
        where = place_t[pl.ds(e, 1), :] - start
        rows = lax.broadcasted_iota(jnp.int32, (SLAB, count), 0)
        pick = (rows == where).astype(F32).astype(BF16)
        one = mult(pick, every[...]).astype(BF16)
        two = mult(pick, across[...]).astype(BF16)
        x = jnp.where(second, two, one)[:, :depth]
        c = jnp.where(second, one, two)[:, :depth]
        x_out[e] = x
        c_out[e] = c
        span = pl.ds(start, SLAB)
        wide = w_gate.shape[2]
        acc[span, 0:wide] += mult(x, w_gate[e])
        acc[span, PIECE : PIECE + wide] += mult(x, w_up[e])
        acc[span, 2 * PIECE : 2 * PIECE + wide] += mult(c, w_down[e], NT)
        return carry

    lax.fori_loop(0, EXP_GROUP, step, 0)
    peers = len(outs)
    chunk = outs[0].shape[0]
    for k in range(peers):
        at = pl.multiple_of(((info[5] * turn + k) % peers) * chunk, 8)
        outs[k][...] = acc[pl.ds(at, chunk), :].astype(outs[k].dtype)


def middle_kernel(info, place_t, gate_t, *rest):
    pieces, out = rest[:-1], rest[-1]
    chunk = out.shape[0]
    count = place_t.shape[1]
    total = pieces[0][...].astype(F32)
    for piece in pieces[1:]:
        total = total + piece[...].astype(F32)
    gate_pre = total[:, :PIECE]
    up_pre = total[:, PIECE : 2 * PIECE]
    dh_raw = total[:, 2 * PIECE :]
    rows = lax.broadcasted_iota(jnp.int32, (chunk, count), 0) + info[5] * chunk
    found = jnp.zeros((chunk, count), F32)
    for e in range(EXP_GROUP):
        found = found + jnp.where(rows == place_t[e : e + 1, :], gate_t[e : e + 1, :], 0.0)
    row_gate = jnp.sum(found, axis=1, keepdims=True)
    sigma = jax.nn.sigmoid(gate_pre)
    silu = gate_pre * sigma
    hidden = silu * up_pre
    dh = dh_raw * row_gate
    d_gate_pre = dh * up_pre * sigma * (1.0 + gate_pre * (1.0 - sigma))
    d_up_pre = dh * silu
    term = jnp.sum(dh_raw * hidden, axis=1, keepdims=True)
    top = term.astype(BF16).astype(F32)
    lanes = lax.broadcasted_iota(jnp.int32, (chunk, PIECE), 1)
    scaled = hidden * row_gate
    scaled = jnp.where(lanes == PIECE - 24, top, scaled)
    scaled = jnp.where(lanes == PIECE - 23, term - top, scaled)
    out[:, :PIECE] = scaled.astype(BF16)
    out[:, PIECE : 2 * PIECE] = d_gate_pre.astype(BF16)
    out[:, 2 * PIECE :] = d_up_pre.astype(BF16)


def tokens_kernel(turn, info, place, every, w_gate, w_up, w_down, *rest):
    chunks, (keep, send, full, acc, laid) = rest[:-5], rest[-5:]
    peers = len(chunks)
    chunk = chunks[0].shape[0]
    for k in range(peers):
        at = pl.multiple_of(((info[5] * turn + k) % peers) * chunk, 8)
        laid[pl.ds(at, chunk), :] = chunks[k][...].astype(F32)
    full[...] = laid[...].astype(BF16)
    count = place.shape[0]
    ff = w_gate.shape[2]
    width = w_gate.shape[1]
    acc[...] = jnp.zeros_like(acc)
    lane = lax.broadcasted_iota(jnp.int32, place.shape, 1)
    here = every[:, PIECE - 128 :].astype(F32).astype(jnp.int32) - info[6] * EXP_GROUP

    def step(e, carry):
        start = slab_of(info, e, laid.shape[0])
        where = jnp.sum(jnp.where(lane == e, place[...], 0), axis=1, keepdims=True) - start
        cols = lax.broadcasted_iota(jnp.int32, (count, SLAB), 1)
        pick = (cols == where).astype(F32).astype(BF16)
        got = mult(pick, full[pl.ds(start, SLAB), :])
        hid = got[:, :PIECE]
        at = lax.broadcasted_iota(jnp.int32, hid.shape, 1)
        term = jnp.sum(jnp.where(at >= ff, hid, 0.0), axis=1, keepdims=True)
        got = got.astype(BF16)
        acc[:, 0:width] += mult(got[:, :ff], w_down[e])
        acc[:, PIECE : PIECE + width] += mult(
            got[:, PIECE : PIECE + ff], w_gate[e], NT
        ) + mult(got[:, 2 * PIECE : 2 * PIECE + ff], w_up[e], NT)
        acc[:, 2 * PIECE : 2 * PIECE + 128] += jnp.where(here == e, term, 0.0)
        return carry

    lax.fori_loop(0, EXP_GROUP, step, 0)
    term = acc[:, 2 * PIECE + 104 : 2 * PIECE + 104 + TOPK]
    top = term.astype(BF16).astype(F32)
    acc[:, PIECE - 24 : PIECE - 24 + TOPK] = top
    acc[:, PIECE - 16 : PIECE - 16 + TOPK] = term - top
    block = send.shape[1]
    mine = info[4]

    def copy(chip, carry):
        a = pl.multiple_of((2 * chip + mine) * block, block)
        b = pl.multiple_of((2 * chip + 1 - mine) * block, block)
        keep[chip] = acc[pl.ds(a, block), 0 : 2 * PIECE]
        send[chip] = acc[pl.ds(b, block), 0 : 2 * PIECE].astype(BF16)
        return carry

    lax.fori_loop(0, send.shape[0], copy, 0)


def join_kernel(keep, got, out):
    total = keep[...] + got[...].astype(F32)
    head = total[:, :, :PIECE]
    term = head[:, :, PIECE - 24 : PIECE - 24 + TOPK] + head[:, :, PIECE - 16 : PIECE - 16 + TOPK]
    top = term.astype(BF16)
    out[...] = total.astype(BF16)
    out[:, :, PIECE - 24 : PIECE - 24 + TOPK] = top
    out[:, :, PIECE - 16 : PIECE - 16 + TOPK] = (term - top.astype(F32)).astype(BF16)


def last_kernel(back, mixed, d_tokens, d_gates):
    total = back[0].astype(F32)
    for p in range(1, back.shape[0]):
        total = total + back[p].astype(F32)
    width = mixed.shape[1]
    mixed[...] = total[:, :width].astype(BF16)
    d_tokens[...] = total[:, PIECE : PIECE + width].astype(BF16)
    d_gates[...] = (
        total[:, PIECE - 24 : PIECE - 24 + TOPK] + total[:, PIECE - 16 : PIECE - 16 + TOPK]
    )


def grads_kernel(info, full, x_rows, c_rows, g_gate, g_up, g_down):
    ff = g_gate.shape[2]

    def step(e, carry):
        start = slab_of(info, e, full.shape[0])
        slab = full[pl.ds(start, SLAB), :]
        x = x_rows[e]
        c = c_rows[e]
        g_gate[e] = mult(x, slab[:, PIECE : PIECE + ff], TN).astype(BF16)
        g_up[e] = mult(x, slab[:, 2 * PIECE : 2 * PIECE + ff], TN).astype(BF16)
        g_down[e] = mult(slab[:, :ff], c, TN).astype(BF16)
        return carry

    lax.fori_loop(0, EXP_GROUP, step, 0)


def called(kernel, outs, n_in, first=SMEM, scratch=()):
    one = not isinstance(outs, (list, tuple))
    return pl.pallas_call(
        kernel,
        out_shape=outs,
        in_specs=[first] + [VMEM] * (n_in - 1),
        out_specs=VMEM if one else [VMEM] * len(outs),
        scratch_shapes=list(scratch),
    )


def of(shape, dtype):
    return jax.ShapeDtypeStruct(shape, dtype)


def passed(value, far):
    peers = lax.axis_size("col")
    return lax.ppermute(value, "col", [(i, (i + far) % peers) for i in range(peers)])


def summed(parts):
    own, p1, p2, p3, p4, m3, m2, m1 = parts
    a4 = passed(p4, 2)
    a3 = passed(p3, 1)
    b3 = passed(m3, -1)
    a1 = passed(p1, 1)
    b1 = passed(m1, -1)
    ahead = (p2 + a3.astype(F32) + a4.astype(F32)).astype(BF16)
    behind = (m2 + b3.astype(F32)).astype(BF16)
    return own, a1, b1, passed(ahead, 2), passed(behind, -2)


def collected(own):
    p2 = passed(own, -2)
    m2 = passed(own, 2)
    p1 = passed(own, -1)
    m1 = passed(own, 1)
    p4 = passed(p2, -2)
    p3 = passed(p2, -1)
    m3 = passed(m2, 1)
    return own, p1, p2, p3, p4, m3, m2, m1


def exchanged(pieces):
    pieces = lax.all_to_all(pieces, "col", 0, 0, tiled=True)
    return [pieces[k] for k in range(pieces.shape[0])]


def routed(rows, hops, every, across, place, place_t, gate_t, info, w_gate, w_up, w_down):
    peers = lax.axis_size("col")
    chunk = rows // peers
    chips = lax.axis_size(PLANE) // 2
    tok = every.shape[0] // (2 * chips)
    depth, ff = w_gate.shape[1:]
    piece = (chunk, 3 * PIECE)
    x_rows, c_rows, *parts = called(
        partial(parts_kernel, int(hops)),
        [of((EXP_GROUP, SLAB, depth), BF16)] * 2
        + [of(piece, F32 if hops and k in (0, 2, 6) else BF16) for k in range(peers)],
        7,
        scratch=[pltpu.VMEM((rows, 3 * PIECE), F32)],
    )(info, every, across, place_t, w_gate, w_up, w_down)
    pieces = summed(parts) if hops else exchanged(jnp.stack(parts))
    own = called(middle_kernel, of(piece, BF16), 3 + len(pieces))(info, place_t, gate_t, *pieces)
    chunks = collected(own) if hops else exchanged(jnp.broadcast_to(own[None], (peers, *piece)))
    keep, send, full = called(
        partial(tokens_kernel, int(hops)),
        [
            of((chips, tok, 2 * PIECE), F32),
            of((chips, tok, 2 * PIECE), BF16),
            of((rows, 3 * PIECE), BF16),
        ],
        6 + peers,
        scratch=[
            pltpu.VMEM((every.shape[0], 3 * PIECE), F32),
            pltpu.VMEM((rows, 3 * PIECE), F32),
        ],
    )(info, place, every, w_gate, w_up, w_down, *chunks)
    got = swapped(send)
    joined = called(join_kernel, of((chips, tok, 2 * PIECE), BF16), 2, first=VMEM)(keep, got)
    back = over_chips(joined)
    g_gate, g_up, g_down = called(
        grads_kernel,
        [of(w_gate.shape, BF16), of(w_up.shape, BF16), of(w_down.shape, BF16)],
        4,
    )(info, full, x_rows, c_rows)
    mixed, d_tokens, d_gates = called(
        last_kernel,
        [of((tok, depth), BF16), of((tok, depth), BF16), of((tok, TOPK), F32)],
        1,
        first=VMEM,
    )(back)
    return mixed, d_tokens, d_gates, g_gate, g_up, g_down


def local(tokens, cotangent, w_gate, w_up, w_down, expert_ids, gates):
    every, across = dispatched(tokens, cotangent, expert_ids, gates)
    count = every.shape[0]
    place, place_t, gate_t, info = pl.pallas_call(
        route_kernel,
        out_shape=[
            of((count, 128), jnp.int32),
            of((8, count), jnp.int32),
            of((8, count), F32),
            of((8,), jnp.int32),
        ],
        in_specs=[VMEM],
        out_specs=[VMEM, VMEM, VMEM, SMEM],
    )(every)
    return lax.switch(
        info[7],
        [lambda *a, size=size: routed(size, size == SIZES[0], *a) for size in SIZES],
        every,
        across,
        place,
        place_t,
        gate_t,
        info,
        w_gate,
        w_up,
        w_down,
    )


def solution(mesh):
    in_specs = (
        P(("expert", "row"), "col"),
        P(("expert", "row"), "col"),
        P("expert", "col", "row"),
        P("expert", "col", "row"),
        P("expert", "row", "col"),
        P(("expert", "row"), None),
        P(("expert", "row"), None),
    )
    out_specs = (
        P(("expert", "row"), "col"),
        P(("expert", "row"), "col"),
        P(("expert", "row"), None),
        P("expert", "col", "row"),
        P("expert", "col", "row"),
        P("expert", "row", "col"),
    )
    return jax.shard_map(local, mesh=mesh, in_specs=in_specs, out_specs=out_specs, check_vma=False)
```

```python
from functools import partial

import jax
import jax.numpy as jnp
from jax import lax
from jax.experimental import pallas as pl
from jax.experimental.pallas import tpu as pltpu
from jax.sharding import PartitionSpec as P

TOPK = 4
EXP_GROUP = 4
PLANE = ("expert", "row")
F32 = jnp.float32
BF16 = jnp.bfloat16


def swapped(value):
    pairs = [(i, i ^ 8) for i in range(lax.axis_size(PLANE))]
    return lax.ppermute(value, PLANE, pairs)


def same_core():
    rows = lax.axis_size("row")
    groups = lax.axis_size("expert")
    return [
        [e * rows + r for e in range(core, groups, 2) for r in range(rows)] for core in range(2)
    ]


def over_chips(value):
    return lax.all_to_all(value, PLANE, 0, 0, axis_index_groups=same_core(), tiled=True)


def dispatched(tokens, cotangent, expert_ids, gates):
    tok = tokens.shape[0]
    keep, send = called(
        pack_kernel, [of((tok, PIECE), BF16), of((tok, PIECE), BF16)], 4, first=VMEM
    )(tokens, cotangent, expert_ids.T, gates.T)
    got = swapped(send)
    second = lax.axis_index("expert") % 2 == 1
    pair = jnp.stack([jnp.where(second, got, keep), jnp.where(second, keep, got)])
    chips = lax.axis_size(PLANE) // 2
    every = over_chips(jnp.broadcast_to(pair[None], (chips, *pair.shape)))
    every = every.reshape(-1, PIECE)
    return every, swapped(every)


SIZES = (704, 768, 1024)
SLAB = 272
MAIN = 256
PIECE = 384
VMEM = pl.BlockSpec(memory_space=pltpu.VMEM)
SMEM = pl.BlockSpec(memory_space=pltpu.SMEM)
NT = (((1,), (1,)), ((), ()))
TN = (((0,), (0,)), ((), ()))


def slab_of(info, e, rows):
    return pl.multiple_of(jnp.minimum((info[e] >> 4) << 4, rows - SLAB), 16)


def mult(a, b, dims=(((1,), (0,)), ((), ()))):
    return lax.dot_general(a, b, dims, preferred_element_type=F32)


def moved(value, first, lanes):
    rows = value.shape[0]
    at = lax.broadcasted_iota(jnp.int32, (rows, lanes), 1)
    src = lax.broadcasted_iota(jnp.int32, (rows, lanes), 0)
    put = (at == src + first).astype(F32).astype(BF16)
    return mult(value.astype(BF16), put, TN)


def pack_kernel(tokens, cotangent, ids_t, gates_t, keep, send):
    width = tokens.shape[1]
    rest = gates_t[...]
    meta = moved(ids_t[...].astype(F32), width, PIECE)
    for part in range(1, 4):
        top = rest.astype(BF16).astype(F32)
        meta = meta + moved(top, width + part * TOPK, PIECE)
        rest = rest - top
    second = lax.axis_index("expert") % 2 == 1
    one = tokens[...].astype(F32)
    two = cotangent[...].astype(F32)
    keep[...] = meta.astype(BF16)
    send[...] = meta.astype(BF16)
    keep[:, :width] = jnp.where(second, two, one).astype(BF16)
    send[:, :width] = jnp.where(second, one, two).astype(BF16)


def route_kernel(every, place, place_t, gate_t, info):
    count = every.shape[0]
    first = PIECE - 24
    groups = lax.axis_size("expert")
    group = lax.axis_index("expert")
    at = lax.broadcasted_iota(jnp.int32, (16, PIECE), 1)
    row = lax.broadcasted_iota(jnp.int32, (16, PIECE), 0)
    meta = mult((at == row + first).astype(F32).astype(BF16), every[...], NT)
    ids = meta[0:TOPK]
    weights = meta[TOPK : 2 * TOPK] + meta[2 * TOPK : 3 * TOPK] + meta[3 * TOPK : 4 * TOPK]
    local_ids = ids - (group * EXP_GROUP).astype(F32)
    sub = lax.broadcasted_iota(jnp.int32, (8, count), 0)
    used = jnp.zeros((8, count), F32)
    gate = jnp.zeros((8, count), F32)
    for e in range(EXP_GROUP):
        hit = local_ids == float(e)
        any_hit = jnp.sum(jnp.where(hit, 1.0, 0.0), axis=0, keepdims=True)
        any_gate = jnp.sum(jnp.where(hit, weights, 0.0), axis=0, keepdims=True)
        used = jnp.where(sub == e, any_hit, used)
        gate = jnp.where(sub == e, any_gate, gate)
    gate_t[...] = gate
    a = lax.broadcasted_iota(jnp.int32, (count, count), 0)
    b = lax.broadcasted_iota(jnp.int32, (count, count), 1)
    ahead = mult(used.astype(BF16), (a < b).astype(F32).astype(BF16))
    begin = jnp.float32(0.0)
    for e in range(EXP_GROUP):
        info[e] = begin.astype(jnp.int32)
        ahead = ahead + jnp.where(sub == e, begin, 0.0)
        begin = begin + jnp.sum(jnp.where(sub == e, used, 0.0))
        info[8 + e] = begin.astype(jnp.int32)
    fullest = jnp.float32(0.0)
    for g in range(groups):
        low = float(g * EXP_GROUP)
        inside = (ids >= low) & (ids < low + EXP_GROUP)
        fullest = jnp.maximum(fullest, jnp.sum(jnp.where(inside, 1.0, 0.0)))
    level = jnp.int32(0)
    for size in SIZES[:-1]:
        level = level + (fullest > float(size)).astype(jnp.int32)
    info[4] = group % 2
    info[5] = lax.axis_index("col")
    info[6] = group
    info[7] = level
    spot = jnp.where(used > 0.0, ahead, -4096.0)
    place_t[...] = spot.astype(jnp.int32)
    high = jnp.floor(spot * (1.0 / 256.0))
    column = moved(high, 0, 128) * 256.0 + moved(spot - high * 256.0, 0, 128)
    place[...] = column.astype(jnp.int32)


def parts_kernel(turn, info, every, across, place_t, w_gate, w_up, w_down, x_out, c_out, *rest):
    outs, acc = rest[:-1], rest[-1]
    depth, wide = w_gate.shape[1:]
    count = every.shape[0]
    second = info[4] == 1
    e = pl.program_id(0)

    @pl.when(e == 0)
    def _():
        acc[...] = jnp.zeros_like(acc)

    start = slab_of(info, e, acc.shape[0])
    where = place_t[pl.ds(e, 1), :] - start
    rows = lax.broadcasted_iota(jnp.int32, (SLAB, count), 0)
    pick = (rows == where).astype(F32).astype(BF16)
    one = mult(pick, every[...]).astype(BF16)
    two = mult(pick, across[...]).astype(BF16)
    x = jnp.where(second, two, one)[:, :depth]
    c = jnp.where(second, one, two)[:, :depth]
    x_out[0] = x
    c_out[0] = c
    span = pl.ds(start, SLAB)
    acc[span, 0:wide] += mult(x, w_gate[0])
    acc[span, PIECE : PIECE + wide] += mult(x, w_up[0])
    acc[span, 2 * PIECE : 2 * PIECE + wide] += mult(c, w_down[0], NT)

    @pl.when(e == EXP_GROUP - 1)
    def _():
        peers = len(outs)
        chunk = outs[0].shape[0]
        for k in range(peers):
            at = pl.multiple_of(((info[5] * turn + k) % peers) * chunk, 8)
            outs[k][...] = acc[pl.ds(at, chunk), :].astype(outs[k].dtype)


def middle(rows, info, place_t, gate_t, pieces):
    chunk = pieces[0].shape[0]
    total = sum(piece.astype(F32) for piece in pieces)
    gate_pre = total[:, :PIECE]
    up_pre = total[:, PIECE : 2 * PIECE]
    dh_raw = total[:, 2 * PIECE :]
    mine = info[5] * chunk + jnp.arange(chunk, dtype=jnp.int32)
    row_gate = sum(
        jnp.sum(jnp.where(place_t[e][None, :] == mine[:, None], gate_t[e][None, :], 0.0), axis=1)
        for e in range(EXP_GROUP)
    )[:, None]
    sigma = jax.nn.sigmoid(gate_pre)
    silu = gate_pre * sigma
    hidden = silu * up_pre
    dh = dh_raw * row_gate
    d_gate_pre = dh * up_pre * sigma * (1.0 + gate_pre * (1.0 - sigma))
    d_up_pre = dh * silu
    term = jnp.sum(dh_raw * hidden, axis=1, keepdims=True)
    top = lax.reduce_precision(term, 8, 7)
    lanes = jnp.arange(PIECE, dtype=jnp.int32)[None, :]
    scaled = hidden * row_gate
    scaled = jnp.where(lanes == PIECE - 24, top, scaled)
    scaled = jnp.where(lanes == PIECE - 23, term - top, scaled)
    return jnp.concatenate(
        [scaled.astype(BF16), d_gate_pre.astype(BF16), d_up_pre.astype(BF16)], axis=1
    )


def tokens_kernel(turn, info, place, every, w_gate, w_up, w_down, *rest):
    chunks, (keep, send, full, acc, laid, y) = rest[:-6], rest[-6:]
    count = place.shape[0]
    width, ff = w_gate.shape[1:]
    e = pl.program_id(0)

    @pl.when(e == 0)
    def _():
        peers = len(chunks)
        chunk = chunks[0].shape[0]
        for k in range(peers):
            at = pl.multiple_of(((info[5] * turn + k) % peers) * chunk, 8)
            laid[pl.ds(at, chunk), :] = chunks[k][...].astype(F32)
        full[...] = laid[...].astype(BF16)
        acc[...] = jnp.zeros_like(acc)
        y[...] = jnp.zeros_like(y)

    start = slab_of(info, e, laid.shape[0])
    slab = full[pl.ds(start, SLAB), :]
    y[:, 0:width] = mult(slab[:, :ff], w_down[0])
    y[:, PIECE : PIECE + width] = mult(slab[:, PIECE : PIECE + ff], w_gate[0], NT) + mult(
        slab[:, 2 * PIECE : 2 * PIECE + ff], w_up[0], NT
    )
    tail = slab[:, PIECE - 128 : PIECE].astype(F32)
    lane = lax.broadcasted_iota(jnp.int32, tail.shape, 1)
    term = jnp.sum(jnp.where(lane >= 104, tail, 0.0), axis=1, keepdims=True)
    spare = lax.broadcasted_iota(jnp.int32, (SLAB, 24), 1)
    y[:, width:PIECE] = jnp.where(spare == e, term, 0.0)
    value = y[...]
    high = value.astype(BF16)
    low = (value - high.astype(F32)).astype(BF16)
    at = lax.broadcasted_iota(jnp.int32, place.shape, 1)
    where = jnp.sum(jnp.where(at == e, place[...], 0), axis=1, keepdims=True) - start
    cols = lax.broadcasted_iota(jnp.int32, (count, MAIN), 1)
    pick = (cols == where).astype(F32).astype(BF16)
    acc[...] += mult(pick, high[:MAIN]) + mult(pick, low[:MAIN])

    @pl.when(info[8 + e] - start > MAIN)
    def _():
        more = lax.broadcasted_iota(jnp.int32, (count, SLAB - MAIN), 1) + MAIN
        pick = (more == where).astype(F32).astype(BF16)
        acc[...] += mult(pick, high[MAIN:]) + mult(pick, low[MAIN:])

    @pl.when(e == EXP_GROUP - 1)
    def _():
        here = every[:, PIECE - 128 :].astype(F32).astype(jnp.int32) - info[6] * EXP_GROUP
        got = acc[:, PIECE - 128 : PIECE]
        spot = lax.broadcasted_iota(jnp.int32, got.shape, 1)
        terms = jnp.zeros_like(got)
        for x in range(EXP_GROUP):
            col = jnp.sum(jnp.where(spot == 104 + x, got, 0.0), axis=1, keepdims=True)
            terms = terms + jnp.where(here == x, col, 0.0)
        chosen = (spot >= 104) & (spot < 104 + TOPK)
        acc[:, PIECE - 128 : PIECE] = jnp.where(chosen, terms, got)
        block = send.shape[1]
        mine = info[4]

        def copy(chip, carry):
            a = pl.multiple_of((2 * chip + mine) * block, block)
            b = pl.multiple_of((2 * chip + 1 - mine) * block, block)
            keep[chip] = acc[pl.ds(a, block), :]
            send[chip] = acc[pl.ds(b, block), :].astype(BF16)
            return carry

        lax.fori_loop(0, send.shape[0], copy, 0)


def grads_kernel(info, full, x_rows, c_rows, g_gate, g_up, g_down):
    ff = g_gate.shape[2]
    e = pl.program_id(0)
    start = slab_of(info, e, full.shape[0])
    slab = full[pl.ds(start, SLAB), :]
    x = x_rows[e]
    g_gate[e] = mult(x, slab[:, PIECE : PIECE + ff], TN).astype(BF16)
    g_up[e] = mult(x, slab[:, 2 * PIECE : 2 * PIECE + ff], TN).astype(BF16)
    g_down[e] = mult(slab[:, :ff], c_rows[e], TN).astype(BF16)


def whole(shape):
    return pl.BlockSpec(shape, lambda e: (0,) * len(shape))


def slice_of(shape):
    return pl.BlockSpec((1, *shape[1:]), lambda e: (e,) + (0,) * (len(shape) - 1))


def by_expert(kernel, outs, args, per, per_out, scratch=()):
    return pl.pallas_call(
        kernel,
        grid=(EXP_GROUP,),
        out_shape=outs,
        in_specs=[SMEM]
        + [
            (slice_of if i in per else whole)(a.shape) for i, a in enumerate(args) if i > 0
        ],
        out_specs=[(slice_of if i in per_out else whole)(o.shape) for i, o in enumerate(outs)],
        scratch_shapes=list(scratch),
    )(*args)


def called(kernel, outs, n_in, first=SMEM, scratch=()):
    one = not isinstance(outs, (list, tuple))
    return pl.pallas_call(
        kernel,
        out_shape=outs,
        in_specs=[first] + [VMEM] * (n_in - 1),
        out_specs=VMEM if one else [VMEM] * len(outs),
        scratch_shapes=list(scratch),
    )


def of(shape, dtype):
    return jax.ShapeDtypeStruct(shape, dtype)


def passed(value, far):
    peers = lax.axis_size("col")
    return lax.ppermute(value, "col", [(i, (i + far) % peers) for i in range(peers)])


def summed(parts):
    own, p1, p2, p3, p4, m3, m2, m1 = parts
    a4 = passed(p4, 2)
    a3 = passed(p3, 1)
    b3 = passed(m3, -1)
    a1 = passed(p1, 1)
    b1 = passed(m1, -1)
    ahead = (p2 + a3.astype(F32) + a4.astype(F32)).astype(BF16)
    behind = (m2 + b3.astype(F32)).astype(BF16)
    return own, a1, b1, passed(ahead, 2), passed(behind, -2)


def collected(own):
    p2 = passed(own, -2)
    m2 = passed(own, 2)
    p1 = passed(own, -1)
    m1 = passed(own, 1)
    p4 = passed(p2, -2)
    p3 = passed(p2, -1)
    m3 = passed(m2, 1)
    return own, p1, p2, p3, p4, m3, m2, m1


def exchanged(pieces):
    pieces = lax.all_to_all(pieces, "col", 0, 0, tiled=True)
    return [pieces[k] for k in range(pieces.shape[0])]


def routed(rows, hops, every, across, place, place_t, gate_t, info, w_gate, w_up, w_down):
    peers = lax.axis_size("col")
    chunk = rows // peers
    chips = lax.axis_size(PLANE) // 2
    tok = every.shape[0] // (2 * chips)
    depth, ff = w_gate.shape[1:]
    piece = (chunk, 3 * PIECE)
    x_rows, c_rows, *parts = by_expert(
        partial(parts_kernel, int(hops)),
        [of((EXP_GROUP, SLAB, depth), BF16)] * 2
        + [of(piece, F32 if hops and k in (0, 2, 6) else BF16) for k in range(peers)],
        (info, every, across, place_t, w_gate, w_up, w_down),
        (4, 5, 6),
        (0, 1),
        [pltpu.VMEM((rows, 3 * PIECE), F32)],
    )
    pieces = summed(parts) if hops else exchanged(jnp.stack(parts))
    own = middle(rows, info, place_t, gate_t, pieces)
    chunks = collected(own) if hops else exchanged(jnp.broadcast_to(own[None], (peers, *piece)))
    keep, send, full = by_expert(
        partial(tokens_kernel, int(hops)),
        [
            of((chips, tok, 2 * PIECE), F32),
            of((chips, tok, 2 * PIECE), BF16),
            of((rows, 3 * PIECE), BF16),
        ],
        (info, place, every, w_gate, w_up, w_down, *chunks),
        (3, 4, 5),
        (),
        [
            pltpu.VMEM((every.shape[0], 2 * PIECE), F32),
            pltpu.VMEM((rows, 3 * PIECE), F32),
            pltpu.VMEM((SLAB, 2 * PIECE), F32),
        ],
    )
    joined = (keep + swapped(send).astype(F32)).astype(BF16)
    back = over_chips(joined)
    g_gate, g_up, g_down = by_expert(
        grads_kernel,
        [of(w_gate.shape, BF16), of(w_up.shape, BF16), of(w_down.shape, BF16)],
        (info, full, x_rows, c_rows),
        (),
        (),
    )
    total = jnp.sum(back.astype(F32), axis=0)
    mixed = total[:, :depth].astype(BF16)
    d_tokens = total[:, PIECE : PIECE + depth].astype(BF16)
    d_gates = total[:, PIECE - 24 : PIECE - 24 + TOPK]
    return mixed, d_tokens, d_gates, g_gate, g_up, g_down


def local(tokens, cotangent, w_gate, w_up, w_down, expert_ids, gates):
    every, across = dispatched(tokens, cotangent, expert_ids, gates)
    count = every.shape[0]
    place, place_t, gate_t, info = pl.pallas_call(
        route_kernel,
        out_shape=[
            of((count, 128), jnp.int32),
            of((8, count), jnp.int32),
            of((8, count), F32),
            of((8 + EXP_GROUP,), jnp.int32),
        ],
        in_specs=[VMEM],
        out_specs=[VMEM, VMEM, VMEM, SMEM],
    )(every)
    return lax.switch(
        info[7],
        [lambda *a, size=size: routed(size, size == SIZES[0], *a) for size in SIZES],
        every,
        across,
        place,
        place_t,
        gate_t,
        info,
        w_gate,
        w_up,
        w_down,
    )


def solution(mesh):
    in_specs = (
        P(("expert", "row"), "col"),
        P(("expert", "row"), "col"),
        P("expert", "col", "row"),
        P("expert", "col", "row"),
        P("expert", "row", "col"),
        P(("expert", "row"), None),
        P(("expert", "row"), None),
    )
    out_specs = (
        P(("expert", "row"), "col"),
        P(("expert", "row"), "col"),
        P(("expert", "row"), None),
        P("expert", "col", "row"),
        P("expert", "col", "row"),
        P("expert", "row", "col"),
    )
    return jax.shard_map(local, mesh=mesh, in_specs=in_specs, out_specs=out_specs, check_vma=False)
```

```python
from functools import partial

import jax
import jax.numpy as jnp
from jax import lax
from jax.experimental import pallas as pl
from jax.experimental.pallas import tpu as pltpu
from jax.sharding import PartitionSpec as P

TOPK = 4
EXP_GROUP = 4
PLANE = ("expert", "row")
F32 = jnp.float32
BF16 = jnp.bfloat16


def swapped(value):
    pairs = [(i, i ^ 8) for i in range(lax.axis_size(PLANE))]
    return lax.ppermute(value, PLANE, pairs)


def same_core():
    rows = lax.axis_size("row")
    groups = lax.axis_size("expert")
    return [
        [e * rows + r for e in range(core, groups, 2) for r in range(rows)] for core in range(2)
    ]


def over_chips(value):
    return lax.all_to_all(value, PLANE, 0, 0, axis_index_groups=same_core(), tiled=True)


def dispatched(tokens, cotangent, expert_ids, gates):
    tok = tokens.shape[0]
    keep, send = called(
        pack_kernel, [of((tok, PIECE), BF16), of((tok, PIECE), BF16)], 4, first=VMEM
    )(tokens, cotangent, expert_ids.T, gates.T)
    got = swapped(send)
    second = lax.axis_index("expert") % 2 == 1
    pair = jnp.stack([jnp.where(second, got, keep), jnp.where(second, keep, got)])
    chips = lax.axis_size(PLANE) // 2
    every = over_chips(jnp.broadcast_to(pair[None], (chips, *pair.shape)))
    every = every.reshape(-1, PIECE)
    return every, swapped(every)


SIZES = (704, 768, 1024)
SLAB = 272
MAIN = 256
PIECE = 384
VMEM = pl.BlockSpec(memory_space=pltpu.VMEM)
SMEM = pl.BlockSpec(memory_space=pltpu.SMEM)
NT = (((1,), (1,)), ((), ()))
TN = (((0,), (0,)), ((), ()))


def slab_of(info, e, rows):
    return pl.multiple_of(jnp.minimum((info[e] >> 4) << 4, rows - SLAB), 16)


def mult(a, b, dims=(((1,), (0,)), ((), ()))):
    return lax.dot_general(a, b, dims, preferred_element_type=F32)


def moved(value, first, lanes):
    rows = value.shape[0]
    at = lax.broadcasted_iota(jnp.int32, (rows, lanes), 1)
    src = lax.broadcasted_iota(jnp.int32, (rows, lanes), 0)
    put = (at == src + first).astype(F32).astype(BF16)
    return mult(value.astype(BF16), put, TN)


def pack_kernel(tokens, cotangent, ids_t, gates_t, keep, send):
    width = tokens.shape[1]
    rest = gates_t[...]
    meta = moved(ids_t[...].astype(F32), width, PIECE)
    for part in range(1, 4):
        top = rest.astype(BF16).astype(F32)
        meta = meta + moved(top, width + part * TOPK, PIECE)
        rest = rest - top
    second = lax.axis_index("expert") % 2 == 1
    one = tokens[...].astype(F32)
    two = cotangent[...].astype(F32)
    keep[...] = meta.astype(BF16)
    send[...] = meta.astype(BF16)
    keep[:, :width] = jnp.where(second, two, one).astype(BF16)
    send[:, :width] = jnp.where(second, one, two).astype(BF16)


def route_kernel(every, place, place_t, gate_t, info):
    count = every.shape[0]
    first = PIECE - 24
    groups = lax.axis_size("expert")
    group = lax.axis_index("expert")
    at = lax.broadcasted_iota(jnp.int32, (16, PIECE), 1)
    row = lax.broadcasted_iota(jnp.int32, (16, PIECE), 0)
    meta = mult((at == row + first).astype(F32).astype(BF16), every[...], NT)
    ids = meta[0:TOPK]
    weights = meta[TOPK : 2 * TOPK] + meta[2 * TOPK : 3 * TOPK] + meta[3 * TOPK : 4 * TOPK]
    local_ids = ids - (group * EXP_GROUP).astype(F32)
    sub = lax.broadcasted_iota(jnp.int32, (8, count), 0)
    used = jnp.zeros((8, count), F32)
    gate = jnp.zeros((8, count), F32)
    for e in range(EXP_GROUP):
        hit = local_ids == float(e)
        any_hit = jnp.sum(jnp.where(hit, 1.0, 0.0), axis=0, keepdims=True)
        any_gate = jnp.sum(jnp.where(hit, weights, 0.0), axis=0, keepdims=True)
        used = jnp.where(sub == e, any_hit, used)
        gate = jnp.where(sub == e, any_gate, gate)
    gate_t[...] = gate
    a = lax.broadcasted_iota(jnp.int32, (count, count), 0)
    b = lax.broadcasted_iota(jnp.int32, (count, count), 1)
    ahead = mult(used.astype(BF16), (a < b).astype(F32).astype(BF16))
    begin = jnp.float32(0.0)
    for e in range(EXP_GROUP):
        info[e] = begin.astype(jnp.int32)
        ahead = ahead + jnp.where(sub == e, begin, 0.0)
        begin = begin + jnp.sum(jnp.where(sub == e, used, 0.0))
        info[8 + e] = begin.astype(jnp.int32)
    fullest = jnp.float32(0.0)
    for g in range(groups):
        low = float(g * EXP_GROUP)
        inside = (ids >= low) & (ids < low + EXP_GROUP)
        fullest = jnp.maximum(fullest, jnp.sum(jnp.where(inside, 1.0, 0.0)))
    level = jnp.int32(0)
    for size in SIZES[:-1]:
        level = level + (fullest > float(size)).astype(jnp.int32)
    info[4] = group % 2
    info[5] = lax.axis_index("col")
    info[6] = group
    info[7] = level
    spot = jnp.where(used > 0.0, ahead, -4096.0)
    place_t[...] = spot.astype(jnp.int32)
    high = jnp.floor(spot * (1.0 / 256.0))
    column = moved(high, 0, 128) * 256.0 + moved(spot - high * 256.0, 0, 128)
    place[...] = column.astype(jnp.int32)


def parts_kernel(turn, info, every, across, place_t, w_gate, w_up, w_down, x_out, c_out, *rest):
    outs, acc = rest[:-1], rest[-1]
    depth, wide = w_gate.shape[1:]
    count = every.shape[0]
    second = info[4] == 1
    e = pl.program_id(0)

    @pl.when(e == 0)
    def _():
        acc[...] = jnp.zeros_like(acc)

    start = slab_of(info, e, acc.shape[0])
    where = place_t[pl.ds(e, 1), :] - start
    rows = lax.broadcasted_iota(jnp.int32, (SLAB, count), 0)
    pick = (rows == where).astype(F32).astype(BF16)
    one = mult(pick, every[...]).astype(BF16)
    two = mult(pick, across[...]).astype(BF16)
    x = jnp.where(second, two, one)[:, :depth]
    c = jnp.where(second, one, two)[:, :depth]
    x_out[0] = x
    c_out[0] = c
    span = pl.ds(start, SLAB)
    acc[span, 0:wide] += mult(x, w_gate[0])
    acc[span, PIECE : PIECE + wide] += mult(x, w_up[0])
    acc[span, 2 * PIECE : 2 * PIECE + wide] += mult(c, w_down[0], NT)

    @pl.when(e == EXP_GROUP - 1)
    def _():
        peers = lax.axis_size("col")
        chunk = outs[0].shape[0]
        left = list(outs)
        for k in range(peers):
            at = pl.multiple_of(((info[5] * turn + k) % peers) * chunk, 8)
            done = 0
            while done < chunk:
                out = left.pop(0)
                out[...] = acc[pl.ds(at + done, out.shape[0]), :].astype(out.dtype)
                done += out.shape[0]


def middle(rows, info, place_t, gate_t, pieces):
    chunk = pieces[0].shape[0]
    total = sum(piece.astype(F32) for piece in pieces)
    gate_pre = total[:, :PIECE]
    up_pre = total[:, PIECE : 2 * PIECE]
    dh_raw = total[:, 2 * PIECE :]
    mine = info[5] * chunk + jnp.arange(chunk, dtype=jnp.int32)
    row_gate = sum(
        jnp.sum(jnp.where(place_t[e][None, :] == mine[:, None], gate_t[e][None, :], 0.0), axis=1)
        for e in range(EXP_GROUP)
    )[:, None]
    sigma = jax.nn.sigmoid(gate_pre)
    silu = gate_pre * sigma
    hidden = silu * up_pre
    dh = dh_raw * row_gate
    d_gate_pre = dh * up_pre * sigma * (1.0 + gate_pre * (1.0 - sigma))
    d_up_pre = dh * silu
    term = jnp.sum(dh_raw * hidden, axis=1, keepdims=True)
    top = lax.reduce_precision(term, 8, 7)
    lanes = jnp.arange(PIECE, dtype=jnp.int32)[None, :]
    scaled = hidden * row_gate
    scaled = jnp.where(lanes == PIECE - 24, top, scaled)
    scaled = jnp.where(lanes == PIECE - 23, term - top, scaled)
    return jnp.concatenate(
        [scaled.astype(BF16), d_gate_pre.astype(BF16), d_up_pre.astype(BF16)], axis=1
    )


def tokens_kernel(turn, info, place, every, w_gate, w_up, w_down, *rest):
    chunks, (keep, send, slabs, acc, laid, y) = rest[:-6], rest[-6:]
    count = place.shape[0]
    width, ff = w_gate.shape[1:]
    e = pl.program_id(0)

    @pl.when(e == 0)
    def _():
        peers = len(chunks)
        chunk = chunks[0].shape[0]
        for k in range(peers):
            at = pl.multiple_of(((info[5] * turn + k) % peers) * chunk, 8)
            laid[pl.ds(at, chunk), :] = chunks[k][...].astype(F32)
        acc[...] = jnp.zeros_like(acc)
        y[...] = jnp.zeros_like(y)

    start = slab_of(info, e, laid.shape[0])
    slab = laid[pl.ds(start, SLAB), :].astype(BF16)
    slabs[e] = slab
    y[:, 0:width] = mult(slab[:, :ff], w_down[0])
    y[:, PIECE : PIECE + width] = mult(slab[:, PIECE : PIECE + ff], w_gate[0], NT) + mult(
        slab[:, 2 * PIECE : 2 * PIECE + ff], w_up[0], NT
    )
    tail = slab[:, PIECE - 128 : PIECE].astype(F32)
    lane = lax.broadcasted_iota(jnp.int32, tail.shape, 1)
    term = jnp.sum(jnp.where(lane >= 104, tail, 0.0), axis=1, keepdims=True)
    spare = lax.broadcasted_iota(jnp.int32, (SLAB, 24), 1)
    y[:, width:PIECE] = jnp.where(spare == e, term, 0.0)
    value = y[...]
    high = value.astype(BF16)
    low = (value - high.astype(F32)).astype(BF16)
    at = lax.broadcasted_iota(jnp.int32, place.shape, 1)
    where = jnp.sum(jnp.where(at == e, place[...], 0), axis=1, keepdims=True) - start
    cols = lax.broadcasted_iota(jnp.int32, (count, MAIN), 1)
    pick = (cols == where).astype(F32).astype(BF16)
    acc[...] += mult(pick, high[:MAIN]) + mult(pick, low[:MAIN])

    @pl.when(info[8 + e] - start > MAIN)
    def _():
        more = lax.broadcasted_iota(jnp.int32, (count, SLAB - MAIN), 1) + MAIN
        pick = (more == where).astype(F32).astype(BF16)
        acc[...] += mult(pick, high[MAIN:]) + mult(pick, low[MAIN:])

    @pl.when(e == EXP_GROUP - 1)
    def _():
        here = every[:, PIECE - 128 :].astype(F32).astype(jnp.int32) - info[6] * EXP_GROUP
        got = acc[:, PIECE - 128 : PIECE]
        spot = lax.broadcasted_iota(jnp.int32, got.shape, 1)
        terms = jnp.zeros_like(got)
        for x in range(EXP_GROUP):
            col = jnp.sum(jnp.where(spot == 104 + x, got, 0.0), axis=1, keepdims=True)
            terms = terms + jnp.where(here == x, col, 0.0)
        chosen = (spot >= 104) & (spot < 104 + TOPK)
        acc[:, PIECE - 128 : PIECE] = jnp.where(chosen, terms, got)
        block = send.shape[1]
        mine = info[4]

        def copy(chip, carry):
            a = pl.multiple_of((2 * chip + mine) * block, block)
            b = pl.multiple_of((2 * chip + 1 - mine) * block, block)
            keep[chip] = acc[pl.ds(a, block), :]
            send[chip] = acc[pl.ds(b, block), :].astype(BF16)
            return carry

        lax.fori_loop(0, send.shape[0], copy, 0)


def grads_kernel(info, slabs, x_rows, c_rows, g_gate, g_up, g_down):
    ff = g_gate.shape[2]
    e = pl.program_id(0)
    slab = slabs[e]
    x = x_rows[e]
    g_gate[e] = mult(x, slab[:, PIECE : PIECE + ff], TN).astype(BF16)
    g_up[e] = mult(x, slab[:, 2 * PIECE : 2 * PIECE + ff], TN).astype(BF16)
    g_down[e] = mult(slab[:, :ff], c_rows[e], TN).astype(BF16)


def whole(shape):
    return pl.BlockSpec(shape, lambda e: (0,) * len(shape))


def slice_of(shape):
    return pl.BlockSpec((1, *shape[1:]), lambda e: (e,) + (0,) * (len(shape) - 1))


def by_expert(kernel, outs, args, per, per_out, scratch=()):
    return pl.pallas_call(
        kernel,
        grid=(EXP_GROUP,),
        out_shape=outs,
        in_specs=[SMEM]
        + [
            (slice_of if i in per else whole)(a.shape) for i, a in enumerate(args) if i > 0
        ],
        out_specs=[(slice_of if i in per_out else whole)(o.shape) for i, o in enumerate(outs)],
        scratch_shapes=list(scratch),
    )(*args)


def called(kernel, outs, n_in, first=SMEM, scratch=()):
    one = not isinstance(outs, (list, tuple))
    return pl.pallas_call(
        kernel,
        out_shape=outs,
        in_specs=[first] + [VMEM] * (n_in - 1),
        out_specs=VMEM if one else [VMEM] * len(outs),
        scratch_shapes=list(scratch),
    )


def of(shape, dtype):
    return jax.ShapeDtypeStruct(shape, dtype)


def passed(value, far):
    peers = lax.axis_size("col")
    return lax.ppermute(value, "col", [(i, (i + far) % peers) for i in range(peers)])


def summed(parts):
    own, p1, p2, p3, p4a, p4b, m3, m2, m1 = parts
    a3 = passed(p3, 1)
    b3 = passed(m3, -1)
    a4 = passed(p4a, 2)
    b4 = passed(p4b, -2)
    a1 = passed(p1, 1)
    b1 = passed(m1, -1)
    low, high = p4a.shape[0], p4b.shape[0]
    a4 = jnp.pad(a4.astype(F32), ((0, high), (0, 0)))
    b4 = jnp.pad(b4.astype(F32), ((low, 0), (0, 0)))
    ahead = (p2 + a3.astype(F32) + a4).astype(BF16)
    behind = (m2 + b3.astype(F32) + b4).astype(BF16)
    return own, a1, b1, passed(ahead, 2), passed(behind, -2)


def collected(own):
    p2 = passed(own, -2)
    m2 = passed(own, 2)
    p1 = passed(own, -1)
    m1 = passed(own, 1)
    p4 = passed(p2, -2)
    p3 = passed(p2, -1)
    m3 = passed(m2, 1)
    return own, p1, p2, p3, p4, m3, m2, m1


def exchanged(pieces):
    pieces = lax.all_to_all(pieces, "col", 0, 0, tiled=True)
    return [pieces[k] for k in range(pieces.shape[0])]


def routed(rows, hops, every, across, place, place_t, gate_t, info, w_gate, w_up, w_down):
    peers = lax.axis_size("col")
    chunk = rows // peers
    chips = lax.axis_size(PLANE) // 2
    tok = every.shape[0] // (2 * chips)
    depth, ff = w_gate.shape[1:]
    piece = (chunk, 3 * PIECE)
    sizes = [of(piece, F32 if hops and k in (0, 2, 6) else BF16) for k in range(peers)]
    if hops:
        top = chunk // 16 * 8
        sizes[4:5] = [of((n, 3 * PIECE), BF16) for n in (top, chunk - top)]
    x_rows, c_rows, *parts = by_expert(
        partial(parts_kernel, int(hops)),
        [of((EXP_GROUP, SLAB, depth), BF16)] * 2
        + sizes,
        (info, every, across, place_t, w_gate, w_up, w_down),
        (4, 5, 6),
        (0, 1),
        [pltpu.VMEM((rows, 3 * PIECE), F32)],
    )
    pieces = summed(parts) if hops else exchanged(jnp.stack(parts))
    own = middle(rows, info, place_t, gate_t, pieces)
    chunks = collected(own) if hops else exchanged(jnp.broadcast_to(own[None], (peers, *piece)))
    keep, send, slabs = by_expert(
        partial(tokens_kernel, int(hops)),
        [
            of((chips, tok, 2 * PIECE), F32),
            of((chips, tok, 2 * PIECE), BF16),
            of((EXP_GROUP, SLAB, 3 * PIECE), BF16),
        ],
        (info, place, every, w_gate, w_up, w_down, *chunks),
        (3, 4, 5),
        (),
        [
            pltpu.VMEM((every.shape[0], 2 * PIECE), F32),
            pltpu.VMEM((rows, 3 * PIECE), F32),
            pltpu.VMEM((SLAB, 2 * PIECE), F32),
        ],
    )
    return keep, send, slabs, x_rows, c_rows


def local(tokens, cotangent, w_gate, w_up, w_down, expert_ids, gates):
    every, across = dispatched(tokens, cotangent, expert_ids, gates)
    count = every.shape[0]
    place, place_t, gate_t, info = pl.pallas_call(
        route_kernel,
        out_shape=[
            of((count, 128), jnp.int32),
            of((8, count), jnp.int32),
            of((8, count), F32),
            of((8 + EXP_GROUP,), jnp.int32),
        ],
        in_specs=[VMEM],
        out_specs=[VMEM, VMEM, VMEM, SMEM],
    )(every)
    keep, send, slabs, x_rows, c_rows = lax.switch(
        info[7],
        [lambda *a, size=size: routed(size, size == SIZES[0], *a) for size in SIZES],
        every,
        across,
        place,
        place_t,
        gate_t,
        info,
        w_gate,
        w_up,
        w_down,
    )
    depth = w_gate.shape[1]
    joined = (keep + swapped(send).astype(F32)).astype(BF16)
    back = over_chips(joined)
    g_gate, g_up, g_down = by_expert(
        grads_kernel,
        [of(w_gate.shape, BF16), of(w_up.shape, BF16), of(w_down.shape, BF16)],
        (info, slabs, x_rows, c_rows),
        (),
        (),
    )
    total = jnp.sum(back.astype(F32), axis=0)
    mixed = total[:, :depth].astype(BF16)
    d_tokens = total[:, PIECE : PIECE + depth].astype(BF16)
    d_gates = total[:, PIECE - 24 : PIECE - 24 + TOPK]
    return mixed, d_tokens, d_gates, g_gate, g_up, g_down


def solution(mesh):
    in_specs = (
        P(("expert", "row"), "col"),
        P(("expert", "row"), "col"),
        P("expert", "col", "row"),
        P("expert", "col", "row"),
        P("expert", "row", "col"),
        P(("expert", "row"), None),
        P(("expert", "row"), None),
    )
    out_specs = (
        P(("expert", "row"), "col"),
        P(("expert", "row"), "col"),
        P(("expert", "row"), None),
        P("expert", "col", "row"),
        P("expert", "col", "row"),
        P("expert", "row", "col"),
    )
    return jax.shard_map(local, mesh=mesh, in_specs=in_specs, out_specs=out_specs, check_vma=False)
```

```python
from functools import partial

import jax
import jax.numpy as jnp
from jax import lax
from jax.experimental import pallas as pl
from jax.experimental.pallas import tpu as pltpu
from jax.sharding import PartitionSpec as P

TOPK = 4
EXP_GROUP = 4
PLANE = ("expert", "row")
F32 = jnp.float32
BF16 = jnp.bfloat16


def swapped(value):
    pairs = [(i, i ^ 8) for i in range(lax.axis_size(PLANE))]
    return lax.ppermute(value, PLANE, pairs)


def same_core():
    rows = lax.axis_size("row")
    groups = lax.axis_size("expert")
    return [
        [e * rows + r for e in range(core, groups, 2) for r in range(rows)] for core in range(2)
    ]


def over_chips(value):
    return lax.all_to_all(value, PLANE, 0, 0, axis_index_groups=same_core(), tiled=True)


def dispatched(tokens, cotangent, expert_ids, gates):
    tok = tokens.shape[0]
    keep, send = called(
        pack_kernel, [of((tok, PIECE), BF16), of((tok, PIECE), BF16)], 4, first=VMEM
    )(tokens, cotangent, expert_ids.T, gates.T)
    got = swapped(send)
    second = lax.axis_index("expert") % 2 == 1
    pair = jnp.stack([jnp.where(second, got, keep), jnp.where(second, keep, got)])
    chips = lax.axis_size(PLANE) // 2
    every = over_chips(jnp.broadcast_to(pair[None], (chips, *pair.shape)))
    every = every.reshape(-1, PIECE)
    return every, swapped(every)


SIZES = (704, 768, 1024)
SLAB = 272
MAIN = 256
PIECE = 384
VMEM = pl.BlockSpec(memory_space=pltpu.VMEM)
SMEM = pl.BlockSpec(memory_space=pltpu.SMEM)
NT = (((1,), (1,)), ((), ()))
TN = (((0,), (0,)), ((), ()))


def slab_of(info, e, rows):
    return pl.multiple_of(jnp.minimum((info[e] >> 4) << 4, rows - SLAB), 16)


def mult(a, b, dims=(((1,), (0,)), ((), ()))):
    return lax.dot_general(a, b, dims, preferred_element_type=F32)


def moved(value, first, lanes):
    rows = value.shape[0]
    at = lax.broadcasted_iota(jnp.int32, (rows, lanes), 1)
    src = lax.broadcasted_iota(jnp.int32, (rows, lanes), 0)
    put = (at == src + first).astype(F32).astype(BF16)
    return mult(value.astype(BF16), put, TN)


def pack_kernel(tokens, cotangent, ids_t, gates_t, keep, send):
    width = tokens.shape[1]
    rest = gates_t[...]
    meta = moved(ids_t[...].astype(F32), width, PIECE)
    for part in range(1, 4):
        top = rest.astype(BF16).astype(F32)
        meta = meta + moved(top, width + part * TOPK, PIECE)
        rest = rest - top
    second = lax.axis_index("expert") % 2 == 1
    one = tokens[...].astype(F32)
    two = cotangent[...].astype(F32)
    keep[...] = meta.astype(BF16)
    send[...] = meta.astype(BF16)
    keep[:, :width] = jnp.where(second, two, one).astype(BF16)
    send[:, :width] = jnp.where(second, one, two).astype(BF16)


def route_kernel(every, place, place_t, gate_t, info):
    count = every.shape[0]
    first = PIECE - 24
    groups = lax.axis_size("expert")
    group = lax.axis_index("expert")
    at = lax.broadcasted_iota(jnp.int32, (16, PIECE), 1)
    row = lax.broadcasted_iota(jnp.int32, (16, PIECE), 0)
    meta = mult((at == row + first).astype(F32).astype(BF16), every[...], NT)
    ids = meta[0:TOPK]
    weights = meta[TOPK : 2 * TOPK] + meta[2 * TOPK : 3 * TOPK] + meta[3 * TOPK : 4 * TOPK]
    local_ids = ids - (group * EXP_GROUP).astype(F32)
    sub = lax.broadcasted_iota(jnp.int32, (8, count), 0)
    used = jnp.zeros((8, count), F32)
    gate = jnp.zeros((8, count), F32)
    for e in range(EXP_GROUP):
        hit = local_ids == float(e)
        any_hit = jnp.sum(jnp.where(hit, 1.0, 0.0), axis=0, keepdims=True)
        any_gate = jnp.sum(jnp.where(hit, weights, 0.0), axis=0, keepdims=True)
        used = jnp.where(sub == e, any_hit, used)
        gate = jnp.where(sub == e, any_gate, gate)
    gate_t[...] = gate
    a = lax.broadcasted_iota(jnp.int32, (count, count), 0)
    b = lax.broadcasted_iota(jnp.int32, (count, count), 1)
    ahead = mult(used.astype(BF16), (a < b).astype(F32).astype(BF16))
    begin = jnp.float32(0.0)
    for e in range(EXP_GROUP):
        info[e] = begin.astype(jnp.int32)
        ahead = ahead + jnp.where(sub == e, begin, 0.0)
        begin = begin + jnp.sum(jnp.where(sub == e, used, 0.0))
        info[8 + e] = begin.astype(jnp.int32)
    fullest = jnp.float32(0.0)
    for g in range(groups):
        low = float(g * EXP_GROUP)
        inside = (ids >= low) & (ids < low + EXP_GROUP)
        fullest = jnp.maximum(fullest, jnp.sum(jnp.where(inside, 1.0, 0.0)))
    level = jnp.int32(0)
    for size in SIZES[:-1]:
        level = level + (fullest > float(size)).astype(jnp.int32)
    info[4] = group % 2
    info[5] = lax.axis_index("col")
    info[6] = group
    info[7] = level
    spot = jnp.where(used > 0.0, ahead, -4096.0)
    place_t[...] = spot.astype(jnp.int32)
    high = jnp.floor(spot * (1.0 / 256.0))
    column = moved(high, 0, 128) * 256.0 + moved(spot - high * 256.0, 0, 128)
    place[...] = column.astype(jnp.int32)


def parts_kernel(turn, info, every, across, place_t, w_gate, w_up, w_down, x_out, c_out, *rest):
    outs, acc = rest[:-1], rest[-1]
    depth, wide = w_gate.shape[1:]
    count = every.shape[0]
    second = info[4] == 1
    e = pl.program_id(0)

    @pl.when(e == 0)
    def _():
        acc[...] = jnp.zeros_like(acc)

    start = slab_of(info, e, acc.shape[0])
    where = place_t[pl.ds(e, 1), :] - start
    rows = lax.broadcasted_iota(jnp.int32, (SLAB, count), 0)
    pick = (rows == where).astype(F32).astype(BF16)
    one = mult(pick, every[...]).astype(BF16)
    two = mult(pick, across[...]).astype(BF16)
    x = jnp.where(second, two, one)[:, :depth]
    c = jnp.where(second, one, two)[:, :depth]
    x_out[0] = x
    c_out[0] = c
    span = pl.ds(start, SLAB)
    acc[span, 0:wide] += mult(x, w_gate[0])
    acc[span, PIECE : PIECE + wide] += mult(x, w_up[0])
    acc[span, 2 * PIECE : 2 * PIECE + wide] += mult(c, w_down[0], NT)

    @pl.when(e == EXP_GROUP - 1)
    def _():
        peers = lax.axis_size("col")
        chunk = outs[0].shape[0]
        left = list(outs)
        for k in range(peers):
            at = pl.multiple_of(((info[5] * turn + k) % peers) * chunk, 8)
            done = 0
            while done < chunk:
                out = left.pop(0)
                out[...] = acc[pl.ds(at + done, out.shape[0]), :].astype(out.dtype)
                done += out.shape[0]


def middle(rows, info, place_t, gate_t, pieces):
    chunk = pieces[0].shape[0]
    total = sum(piece.astype(F32) for piece in pieces)
    gate_pre = total[:, :PIECE]
    up_pre = total[:, PIECE : 2 * PIECE]
    dh_raw = total[:, 2 * PIECE :]
    mine = info[5] * chunk + jnp.arange(chunk, dtype=jnp.int32)
    row_gate = sum(
        jnp.sum(jnp.where(place_t[e][None, :] == mine[:, None], gate_t[e][None, :], 0.0), axis=1)
        for e in range(EXP_GROUP)
    )[:, None]
    sigma = jax.nn.sigmoid(gate_pre)
    silu = gate_pre * sigma
    hidden = silu * up_pre
    dh = dh_raw * row_gate
    d_gate_pre = dh * up_pre * sigma * (1.0 + gate_pre * (1.0 - sigma))
    d_up_pre = dh * silu
    term = jnp.sum(dh_raw * hidden, axis=1, keepdims=True)
    top = lax.reduce_precision(term, 8, 7)
    lanes = jnp.arange(PIECE, dtype=jnp.int32)[None, :]
    scaled = hidden * row_gate
    scaled = jnp.where(lanes == PIECE - 24, top, scaled)
    scaled = jnp.where(lanes == PIECE - 23, term - top, scaled)
    return jnp.concatenate(
        [scaled.astype(BF16), d_gate_pre.astype(BF16), d_up_pre.astype(BF16)], axis=1
    )


def tokens_kernel(turn, info, place, every, w_gate, w_up, w_down, *rest):
    chunks, (keep, send, slabs, acc, laid, y) = rest[:-6], rest[-6:]
    count = place.shape[0]
    width, ff = w_gate.shape[1:]
    e = pl.program_id(0)

    @pl.when(e == 0)
    def _():
        peers = len(chunks)
        chunk = chunks[0].shape[0]
        for k in range(peers):
            at = pl.multiple_of(((info[5] * turn + k) % peers) * chunk, 8)
            laid[pl.ds(at, chunk), :] = chunks[k][...].astype(F32)
        acc[...] = jnp.zeros_like(acc)
        y[...] = jnp.zeros_like(y)

    start = slab_of(info, e, laid.shape[0])
    slab = laid[pl.ds(start, SLAB), :].astype(BF16)
    slabs[e] = slab
    y[:, 0:width] = mult(slab[:, :ff], w_down[0])
    y[:, PIECE : PIECE + width] = mult(slab[:, PIECE : PIECE + ff], w_gate[0], NT) + mult(
        slab[:, 2 * PIECE : 2 * PIECE + ff], w_up[0], NT
    )
    tail = slab[:, PIECE - 128 : PIECE].astype(F32)
    lane = lax.broadcasted_iota(jnp.int32, tail.shape, 1)
    term = jnp.sum(jnp.where(lane >= 104, tail, 0.0), axis=1, keepdims=True)
    spare = lax.broadcasted_iota(jnp.int32, (SLAB, 24), 1)
    y[:, width:PIECE] = jnp.where(spare == e, term, 0.0)
    value = y[...]
    high = value.astype(BF16)
    low = (value - high.astype(F32)).astype(BF16)
    at = lax.broadcasted_iota(jnp.int32, place.shape, 1)
    where = jnp.sum(jnp.where(at == e, place[...], 0), axis=1, keepdims=True) - start
    cols = lax.broadcasted_iota(jnp.int32, (count, MAIN), 1)
    pick = (cols == where).astype(F32).astype(BF16)
    acc[...] += mult(pick, high[:MAIN]) + mult(pick, low[:MAIN])

    @pl.when(info[8 + e] - start > MAIN)
    def _():
        more = lax.broadcasted_iota(jnp.int32, (count, SLAB - MAIN), 1) + MAIN
        pick = (more == where).astype(F32).astype(BF16)
        acc[...] += mult(pick, high[MAIN:]) + mult(pick, low[MAIN:])

    @pl.when(e == EXP_GROUP - 1)
    def _():
        here = every[:, PIECE - 128 :].astype(F32).astype(jnp.int32) - info[6] * EXP_GROUP
        got = acc[:, PIECE - 128 : PIECE]
        spot = lax.broadcasted_iota(jnp.int32, got.shape, 1)
        terms = jnp.zeros_like(got)
        for x in range(EXP_GROUP):
            col = jnp.sum(jnp.where(spot == 104 + x, got, 0.0), axis=1, keepdims=True)
            terms = terms + jnp.where(here == x, col, 0.0)
        chosen = (spot >= 104) & (spot < 104 + TOPK)
        acc[:, PIECE - 128 : PIECE] = jnp.where(chosen, terms, got)
        block = send.shape[1]
        mine = info[4]

        def copy(chip, carry):
            a = pl.multiple_of((2 * chip + mine) * block, block)
            b = pl.multiple_of((2 * chip + 1 - mine) * block, block)
            keep[chip] = acc[pl.ds(a, block), :]
            send[chip] = acc[pl.ds(b, block), :].astype(BF16)
            return carry

        lax.fori_loop(0, send.shape[0], copy, 0)


def grads_kernel(info, slabs, x_rows, c_rows, g_gate, g_up, g_down):
    ff = g_gate.shape[2]
    e = pl.program_id(0)
    slab = slabs[e]
    x = x_rows[e]
    g_gate[e] = mult(x, slab[:, PIECE : PIECE + ff], TN).astype(BF16)
    g_up[e] = mult(x, slab[:, 2 * PIECE : 2 * PIECE + ff], TN).astype(BF16)
    g_down[e] = mult(slab[:, :ff], c_rows[e], TN).astype(BF16)


def whole(shape):
    return pl.BlockSpec(shape, lambda e: (0,) * len(shape))


def slice_of(shape):
    return pl.BlockSpec((1, *shape[1:]), lambda e: (e,) + (0,) * (len(shape) - 1))


def by_expert(kernel, outs, args, per, per_out, scratch=()):
    return pl.pallas_call(
        kernel,
        grid=(EXP_GROUP,),
        out_shape=outs,
        in_specs=[SMEM]
        + [
            (slice_of if i in per else whole)(a.shape) for i, a in enumerate(args) if i > 0
        ],
        out_specs=[(slice_of if i in per_out else whole)(o.shape) for i, o in enumerate(outs)],
        scratch_shapes=list(scratch),
    )(*args)


def called(kernel, outs, n_in, first=SMEM, scratch=()):
    one = not isinstance(outs, (list, tuple))
    return pl.pallas_call(
        kernel,
        out_shape=outs,
        in_specs=[first] + [VMEM] * (n_in - 1),
        out_specs=VMEM if one else [VMEM] * len(outs),
        scratch_shapes=list(scratch),
    )


def of(shape, dtype):
    return jax.ShapeDtypeStruct(shape, dtype)


def passed(value, far):
    peers = lax.axis_size("col")
    return lax.ppermute(value, "col", [(i, (i + far) % peers) for i in range(peers)])


def summed(parts):
    own, p1, p2, p3, p4a, p4b, m3, m2, m1 = parts
    a3 = passed(p3, 1)
    b3 = passed(m3, -1)
    a4 = passed(p4a, 2)
    b4 = passed(p4b, -2)
    low, high = p4a.shape[0], p4b.shape[0]
    a4 = jnp.pad(a4.astype(F32), ((0, high), (0, 0)))
    b4 = jnp.pad(b4.astype(F32), ((low, 0), (0, 0)))
    ahead = (p2 + a3.astype(F32) + a4).astype(BF16)
    behind = (m2 + b3.astype(F32) + b4).astype(BF16)
    ahead, p1 = lax.optimization_barrier((ahead, p1))
    behind, m1 = lax.optimization_barrier((behind, m1))
    return own, passed(ahead, 2), passed(behind, -2), passed(p1, 1), passed(m1, -1)


def collected(own):
    p2 = passed(own, -2)
    m2 = passed(own, 2)
    p1 = passed(own, -1)
    m1 = passed(own, 1)
    p4 = passed(p2, -2)
    p3 = passed(p2, -1)
    m3 = passed(m2, 1)
    return own, p1, p2, p3, p4, m3, m2, m1


def exchanged(pieces):
    pieces = lax.all_to_all(pieces, "col", 0, 0, tiled=True)
    return [pieces[k] for k in range(pieces.shape[0])]


def routed(rows, hops, every, across, place, place_t, gate_t, info, w_gate, w_up, w_down):
    peers = lax.axis_size("col")
    chunk = rows // peers
    chips = lax.axis_size(PLANE) // 2
    tok = every.shape[0] // (2 * chips)
    depth, ff = w_gate.shape[1:]
    piece = (chunk, 3 * PIECE)
    sizes = [of(piece, F32 if hops and k in (0, 2, 6) else BF16) for k in range(peers)]
    if hops:
        top = chunk // 16 * 8
        sizes[4:5] = [of((n, 3 * PIECE), BF16) for n in (top, chunk - top)]
    x_rows, c_rows, *parts = by_expert(
        partial(parts_kernel, int(hops)),
        [of((EXP_GROUP, SLAB, depth), BF16)] * 2
        + sizes,
        (info, every, across, place_t, w_gate, w_up, w_down),
        (4, 5, 6),
        (0, 1),
        [pltpu.VMEM((rows, 3 * PIECE), F32)],
    )
    pieces = summed(parts) if hops else exchanged(jnp.stack(parts))
    own = middle(rows, info, place_t, gate_t, pieces)
    chunks = collected(own) if hops else exchanged(jnp.broadcast_to(own[None], (peers, *piece)))
    keep, send, slabs = by_expert(
        partial(tokens_kernel, int(hops)),
        [
            of((chips, tok, 2 * PIECE), F32),
            of((chips, tok, 2 * PIECE), BF16),
            of((EXP_GROUP, SLAB, 3 * PIECE), BF16),
        ],
        (info, place, every, w_gate, w_up, w_down, *chunks),
        (3, 4, 5),
        (),
        [
            pltpu.VMEM((every.shape[0], 2 * PIECE), F32),
            pltpu.VMEM((rows, 3 * PIECE), F32),
            pltpu.VMEM((SLAB, 2 * PIECE), F32),
        ],
    )
    return keep, send, slabs, x_rows, c_rows


def local(tokens, cotangent, w_gate, w_up, w_down, expert_ids, gates):
    every, across = dispatched(tokens, cotangent, expert_ids, gates)
    count = every.shape[0]
    place, place_t, gate_t, info = pl.pallas_call(
        route_kernel,
        out_shape=[
            of((count, 128), jnp.int32),
            of((8, count), jnp.int32),
            of((8, count), F32),
            of((8 + EXP_GROUP,), jnp.int32),
        ],
        in_specs=[VMEM],
        out_specs=[VMEM, VMEM, VMEM, SMEM],
    )(every)
    keep, send, slabs, x_rows, c_rows = lax.switch(
        info[7],
        [lambda *a, size=size: routed(size, size == SIZES[0], *a) for size in SIZES],
        every,
        across,
        place,
        place_t,
        gate_t,
        info,
        w_gate,
        w_up,
        w_down,
    )
    depth = w_gate.shape[1]
    joined = (keep + swapped(send).astype(F32)).astype(BF16)
    back = over_chips(joined)
    g_gate, g_up, g_down = by_expert(
        grads_kernel,
        [of(w_gate.shape, BF16), of(w_up.shape, BF16), of(w_down.shape, BF16)],
        (info, slabs, x_rows, c_rows),
        (),
        (),
    )
    total = jnp.sum(back.astype(F32), axis=0)
    mixed = total[:, :depth].astype(BF16)
    d_tokens = total[:, PIECE : PIECE + depth].astype(BF16)
    d_gates = total[:, PIECE - 24 : PIECE - 24 + TOPK]
    return mixed, d_tokens, d_gates, g_gate, g_up, g_down


def solution(mesh):
    in_specs = (
        P(("expert", "row"), "col"),
        P(("expert", "row"), "col"),
        P("expert", "col", "row"),
        P("expert", "col", "row"),
        P("expert", "row", "col"),
        P(("expert", "row"), None),
        P(("expert", "row"), None),
    )
    out_specs = (
        P(("expert", "row"), "col"),
        P(("expert", "row"), "col"),
        P(("expert", "row"), None),
        P("expert", "col", "row"),
        P("expert", "col", "row"),
        P("expert", "row", "col"),
    )
    return jax.shard_map(local, mesh=mesh, in_specs=in_specs, out_specs=out_specs, check_vma=False)
```

```python
from functools import partial

import jax
import jax.numpy as jnp
from jax import lax
from jax.experimental import pallas as pl
from jax.experimental.pallas import tpu as pltpu
from jax.sharding import PartitionSpec as P

TOPK = 4
EXP_GROUP = 4
PLANE = ("expert", "row")
F32 = jnp.float32
BF16 = jnp.bfloat16


def swapped(value):
    pairs = [(i, i ^ 8) for i in range(lax.axis_size(PLANE))]
    return lax.ppermute(value, PLANE, pairs)


def same_core():
    rows = lax.axis_size("row")
    groups = lax.axis_size("expert")
    return [
        [e * rows + r for e in range(core, groups, 2) for r in range(rows)] for core in range(2)
    ]


def over_chips(value):
    return lax.all_to_all(value, PLANE, 0, 0, axis_index_groups=same_core(), tiled=True)


def dispatched(tokens, cotangent, expert_ids, gates):
    tok = tokens.shape[0]
    keep, send = called(
        pack_kernel, [of((tok, PIECE), BF16), of((tok, PIECE), BF16)], 4, first=VMEM
    )(tokens, cotangent, expert_ids.T, gates.T)
    got = swapped(send)
    second = lax.axis_index("expert") % 2 == 1
    pair = jnp.stack([jnp.where(second, got, keep), jnp.where(second, keep, got)])
    chips = lax.axis_size(PLANE) // 2
    every = over_chips(jnp.broadcast_to(pair[None], (chips, *pair.shape)))
    every = every.reshape(-1, PIECE)
    return every, swapped(every)


SIZES = (704, 768, 1024)
SLAB = 272
MAIN = 256
PIECE = 384
VMEM = pl.BlockSpec(memory_space=pltpu.VMEM)
SMEM = pl.BlockSpec(memory_space=pltpu.SMEM)
NT = (((1,), (1,)), ((), ()))
TN = (((0,), (0,)), ((), ()))


def slab_of(info, e, rows):
    return pl.multiple_of(jnp.minimum((info[e] >> 4) << 4, rows - SLAB), 16)


def mult(a, b, dims=(((1,), (0,)), ((), ()))):
    return lax.dot_general(a, b, dims, preferred_element_type=F32)


def moved(value, first, lanes):
    rows = value.shape[0]
    at = lax.broadcasted_iota(jnp.int32, (rows, lanes), 1)
    src = lax.broadcasted_iota(jnp.int32, (rows, lanes), 0)
    put = (at == src + first).astype(F32).astype(BF16)
    return mult(value.astype(BF16), put, TN)


def pack_kernel(tokens, cotangent, ids_t, gates_t, keep, send):
    width = tokens.shape[1]
    rest = gates_t[...]
    meta = moved(ids_t[...].astype(F32), width, PIECE)
    for part in range(1, 4):
        top = rest.astype(BF16).astype(F32)
        meta = meta + moved(top, width + part * TOPK, PIECE)
        rest = rest - top
    second = lax.axis_index("expert") % 2 == 1
    one = tokens[...].astype(F32)
    two = cotangent[...].astype(F32)
    keep[...] = meta.astype(BF16)
    send[...] = meta.astype(BF16)
    keep[:, :width] = jnp.where(second, two, one).astype(BF16)
    send[:, :width] = jnp.where(second, one, two).astype(BF16)


def route_kernel(every, place, place_t, gate_t, info):
    count = every.shape[0]
    first = PIECE - 24
    groups = lax.axis_size("expert")
    group = lax.axis_index("expert")
    at = lax.broadcasted_iota(jnp.int32, (16, PIECE), 1)
    row = lax.broadcasted_iota(jnp.int32, (16, PIECE), 0)
    meta = mult((at == row + first).astype(F32).astype(BF16), every[...], NT)
    ids = meta[0:TOPK]
    weights = meta[TOPK : 2 * TOPK] + meta[2 * TOPK : 3 * TOPK] + meta[3 * TOPK : 4 * TOPK]
    local_ids = ids - (group * EXP_GROUP).astype(F32)
    sub = lax.broadcasted_iota(jnp.int32, (8, count), 0)
    used = jnp.zeros((8, count), F32)
    gate = jnp.zeros((8, count), F32)
    for e in range(EXP_GROUP):
        hit = local_ids == float(e)
        any_hit = jnp.sum(jnp.where(hit, 1.0, 0.0), axis=0, keepdims=True)
        any_gate = jnp.sum(jnp.where(hit, weights, 0.0), axis=0, keepdims=True)
        used = jnp.where(sub == e, any_hit, used)
        gate = jnp.where(sub == e, any_gate, gate)
    gate_t[...] = gate
    a = lax.broadcasted_iota(jnp.int32, (count, count), 0)
    b = lax.broadcasted_iota(jnp.int32, (count, count), 1)
    ahead = mult(used.astype(BF16), (a < b).astype(F32).astype(BF16))
    begin = jnp.float32(0.0)
    for e in range(EXP_GROUP):
        info[e] = begin.astype(jnp.int32)
        ahead = ahead + jnp.where(sub == e, begin, 0.0)
        begin = begin + jnp.sum(jnp.where(sub == e, used, 0.0))
        info[8 + e] = begin.astype(jnp.int32)
    fullest = jnp.float32(0.0)
    for g in range(groups):
        low = float(g * EXP_GROUP)
        inside = (ids >= low) & (ids < low + EXP_GROUP)
        fullest = jnp.maximum(fullest, jnp.sum(jnp.where(inside, 1.0, 0.0)))
    level = jnp.int32(0)
    for size in SIZES[:-1]:
        level = level + (fullest > float(size)).astype(jnp.int32)
    info[4] = group % 2
    info[5] = lax.axis_index("col")
    info[6] = group
    info[7] = level
    spot = jnp.where(used > 0.0, ahead, -4096.0)
    place_t[...] = spot.astype(jnp.int32)
    high = jnp.floor(spot * (1.0 / 256.0))
    column = moved(high, 0, 128) * 256.0 + moved(spot - high * 256.0, 0, 128)
    place[...] = column.astype(jnp.int32)


def parts_kernel(turn, info, every, across, place_t, w_gate, w_up, w_down, x_out, c_out, *rest):
    outs, acc = rest[:-1], rest[-1]
    depth, wide = w_gate.shape[1:]
    count = every.shape[0]
    second = info[4] == 1
    e = pl.program_id(0)

    @pl.when(e == 0)
    def _():
        acc[...] = jnp.zeros_like(acc)

    start = slab_of(info, e, acc.shape[0])
    where = place_t[pl.ds(e, 1), :] - start
    rows = lax.broadcasted_iota(jnp.int32, (SLAB, count), 0)
    pick = (rows == where).astype(F32).astype(BF16)
    one = mult(pick, every[...]).astype(BF16)
    two = mult(pick, across[...]).astype(BF16)
    x = jnp.where(second, two, one)[:, :depth]
    c = jnp.where(second, one, two)[:, :depth]
    x_out[0] = x
    c_out[0] = c
    span = pl.ds(start, SLAB)
    acc[span, 0:wide] += mult(x, w_gate[0])
    acc[span, PIECE : PIECE + wide] += mult(x, w_up[0])
    acc[span, 2 * PIECE : 2 * PIECE + wide] += mult(c, w_down[0], NT)

    @pl.when(e == EXP_GROUP - 1)
    def _():
        peers = len(outs)
        chunk = outs[0].shape[0]
        for k in range(peers):
            at = pl.multiple_of(((info[5] * turn + k) % peers) * chunk, 8)
            outs[k][...] = acc[pl.ds(at, chunk), :].astype(outs[k].dtype)


def middle(rows, info, place_t, gate_t, pieces):
    chunk = pieces[0].shape[0]
    total = sum(piece.astype(F32) for piece in pieces)
    gate_pre = total[:, :PIECE]
    up_pre = total[:, PIECE : 2 * PIECE]
    dh_raw = total[:, 2 * PIECE :]
    mine = info[5] * chunk + jnp.arange(chunk, dtype=jnp.int32)
    row_gate = sum(
        jnp.sum(jnp.where(place_t[e][None, :] == mine[:, None], gate_t[e][None, :], 0.0), axis=1)
        for e in range(EXP_GROUP)
    )[:, None]
    sigma = jax.nn.sigmoid(gate_pre)
    silu = gate_pre * sigma
    hidden = silu * up_pre
    dh = dh_raw * row_gate
    d_gate_pre = dh * up_pre * sigma * (1.0 + gate_pre * (1.0 - sigma))
    d_up_pre = dh * silu
    term = jnp.sum(dh_raw * hidden, axis=1, keepdims=True)
    top = lax.reduce_precision(term, 8, 7)
    lanes = jnp.arange(PIECE, dtype=jnp.int32)[None, :]
    scaled = hidden * row_gate
    scaled = jnp.where(lanes == PIECE - 24, top, scaled)
    scaled = jnp.where(lanes == PIECE - 23, term - top, scaled)
    return jnp.concatenate(
        [scaled.astype(BF16), d_gate_pre.astype(BF16), d_up_pre.astype(BF16)], axis=1
    )


def tokens_kernel(turn, info, place, every, w_gate, w_up, w_down, *rest):
    chunks, (keep, send, full, acc, laid, y) = rest[:-6], rest[-6:]
    count = place.shape[0]
    width, ff = w_gate.shape[1:]
    e = pl.program_id(0)

    @pl.when(e == 0)
    def _():
        peers = len(chunks)
        chunk = chunks[0].shape[0]
        for k in range(peers):
            at = pl.multiple_of(((info[5] * turn + k) % peers) * chunk, 8)
            laid[pl.ds(at, chunk), :] = chunks[k][...].astype(F32)
        full[...] = laid[...].astype(BF16)
        acc[...] = jnp.zeros_like(acc)
        y[...] = jnp.zeros_like(y)

    start = slab_of(info, e, laid.shape[0])
    slab = full[pl.ds(start, SLAB), :]
    y[:, 0:width] = mult(slab[:, :ff], w_down[0])
    y[:, PIECE : PIECE + width] = mult(slab[:, PIECE : PIECE + ff], w_gate[0], NT) + mult(
        slab[:, 2 * PIECE : 2 * PIECE + ff], w_up[0], NT
    )
    tail = slab[:, PIECE - 128 : PIECE].astype(F32)
    lane = lax.broadcasted_iota(jnp.int32, tail.shape, 1)
    term = jnp.sum(jnp.where(lane >= 104, tail, 0.0), axis=1, keepdims=True)
    spare = lax.broadcasted_iota(jnp.int32, (SLAB, 24), 1)
    y[:, width:PIECE] = jnp.where(spare == e, term, 0.0)
    value = y[...]
    high = value.astype(BF16)
    low = (value - high.astype(F32)).astype(BF16)
    at = lax.broadcasted_iota(jnp.int32, place.shape, 1)
    where = jnp.sum(jnp.where(at == e, place[...], 0), axis=1, keepdims=True) - start
    cols = lax.broadcasted_iota(jnp.int32, (count, MAIN), 1)
    pick = (cols == where).astype(F32).astype(BF16)
    acc[...] += mult(pick, high[:MAIN]) + mult(pick, low[:MAIN])

    @pl.when(info[8 + e] - start > MAIN)
    def _():
        more = lax.broadcasted_iota(jnp.int32, (count, SLAB - MAIN), 1) + MAIN
        pick = (more == where).astype(F32).astype(BF16)
        acc[...] += mult(pick, high[MAIN:]) + mult(pick, low[MAIN:])

    @pl.when(e == EXP_GROUP - 1)
    def _():
        here = every[:, PIECE - 128 :].astype(F32).astype(jnp.int32) - info[6] * EXP_GROUP
        got = acc[:, PIECE - 128 : PIECE]
        spot = lax.broadcasted_iota(jnp.int32, got.shape, 1)
        terms = jnp.zeros_like(got)
        for x in range(EXP_GROUP):
            col = jnp.sum(jnp.where(spot == 104 + x, got, 0.0), axis=1, keepdims=True)
            terms = terms + jnp.where(here == x, col, 0.0)
        chosen = (spot >= 104) & (spot < 104 + TOPK)
        acc[:, PIECE - 128 : PIECE] = jnp.where(chosen, terms, got)
        block = send.shape[1]
        mine = info[4]

        def copy(chip, carry):
            a = pl.multiple_of((2 * chip + mine) * block, block)
            b = pl.multiple_of((2 * chip + 1 - mine) * block, block)
            keep[chip] = acc[pl.ds(a, block), :]
            send[chip] = acc[pl.ds(b, block), :].astype(BF16)
            return carry

        lax.fori_loop(0, send.shape[0], copy, 0)


def grads_kernel(info, full, x_rows, c_rows, g_gate, g_up, g_down):
    ff = g_gate.shape[2]
    e = pl.program_id(0)
    start = slab_of(info, e, full.shape[0])
    slab = full[pl.ds(start, SLAB), :]
    x = x_rows[e]
    g_gate[e] = mult(x, slab[:, PIECE : PIECE + ff], TN).astype(BF16)
    g_up[e] = mult(x, slab[:, 2 * PIECE : 2 * PIECE + ff], TN).astype(BF16)
    g_down[e] = mult(slab[:, :ff], c_rows[e], TN).astype(BF16)


def whole(shape):
    return pl.BlockSpec(shape, lambda e: (0,) * len(shape))


def slice_of(shape):
    return pl.BlockSpec((1, *shape[1:]), lambda e: (e,) + (0,) * (len(shape) - 1))


def by_expert(kernel, outs, args, per, per_out, scratch=()):
    return pl.pallas_call(
        kernel,
        grid=(EXP_GROUP,),
        out_shape=outs,
        in_specs=[SMEM]
        + [
            (slice_of if i in per else whole)(a.shape) for i, a in enumerate(args) if i > 0
        ],
        out_specs=[(slice_of if i in per_out else whole)(o.shape) for i, o in enumerate(outs)],
        scratch_shapes=list(scratch),
    )(*args)


def called(kernel, outs, n_in, first=SMEM, scratch=()):
    one = not isinstance(outs, (list, tuple))
    return pl.pallas_call(
        kernel,
        out_shape=outs,
        in_specs=[first] + [VMEM] * (n_in - 1),
        out_specs=VMEM if one else [VMEM] * len(outs),
        scratch_shapes=list(scratch),
    )


def of(shape, dtype):
    return jax.ShapeDtypeStruct(shape, dtype)


def passed(value, far):
    peers = lax.axis_size("col")
    return lax.ppermute(value, "col", [(i, (i + far) % peers) for i in range(peers)])


def summed(parts):
    own, p1, p2, p3, p4, m3, m2, m1 = parts
    a4 = passed(p4, 2)
    a3 = passed(p3, 1)
    b3 = passed(m3, -1)
    behind = (m2 + b3.astype(F32)).astype(BF16)
    a4, _ = lax.optimization_barrier((a4, behind))
    behind = passed(behind, -2)
    ahead = passed((p2 + a3.astype(F32) + a4.astype(F32)).astype(BF16), 2)
    return own, passed(p1, 1), passed(m1, -1), ahead, behind


def collected(own):
    p2 = passed(own, -2)
    m2 = passed(own, 2)
    p1 = passed(own, -1)
    m1 = passed(own, 1)
    p4 = passed(p2, -2)
    p3 = passed(p2, -1)
    m3 = passed(m2, 1)
    return own, p1, p2, p3, p4, m3, m2, m1


def exchanged(pieces):
    pieces = lax.all_to_all(pieces, "col", 0, 0, tiled=True)
    return [pieces[k] for k in range(pieces.shape[0])]


def routed(rows, hops, every, across, place, place_t, gate_t, info, w_gate, w_up, w_down):
    peers = lax.axis_size("col")
    chunk = rows // peers
    chips = lax.axis_size(PLANE) // 2
    tok = every.shape[0] // (2 * chips)
    depth, ff = w_gate.shape[1:]
    piece = (chunk, 3 * PIECE)
    x_rows, c_rows, *parts = by_expert(
        partial(parts_kernel, int(hops)),
        [of((EXP_GROUP, SLAB, depth), BF16)] * 2
        + [of(piece, F32 if hops and k in (0, 2, 6) else BF16) for k in range(peers)],
        (info, every, across, place_t, w_gate, w_up, w_down),
        (4, 5, 6),
        (0, 1),
        [pltpu.VMEM((rows, 3 * PIECE), F32)],
    )
    pieces = summed(parts) if hops else exchanged(jnp.stack(parts))
    own = middle(rows, info, place_t, gate_t, pieces)
    chunks = collected(own) if hops else exchanged(jnp.broadcast_to(own[None], (peers, *piece)))
    keep, send, full = by_expert(
        partial(tokens_kernel, int(hops)),
        [
            of((chips, tok, 2 * PIECE), F32),
            of((chips, tok, 2 * PIECE), BF16),
            of((rows, 3 * PIECE), BF16),
        ],
        (info, place, every, w_gate, w_up, w_down, *chunks),
        (3, 4, 5),
        (),
        [
            pltpu.VMEM((every.shape[0], 2 * PIECE), F32),
            pltpu.VMEM((rows, 3 * PIECE), F32),
            pltpu.VMEM((SLAB, 2 * PIECE), F32),
        ],
    )
    joined = (keep + swapped(send).astype(F32)).astype(BF16)
    back = over_chips(joined)
    g_gate, g_up, g_down = by_expert(
        grads_kernel,
        [of(w_gate.shape, BF16), of(w_up.shape, BF16), of(w_down.shape, BF16)],
        (info, full, x_rows, c_rows),
        (),
        (),
    )
    total = jnp.sum(back.astype(F32), axis=0)
    mixed = total[:, :depth].astype(BF16)
    d_tokens = total[:, PIECE : PIECE + depth].astype(BF16)
    d_gates = total[:, PIECE - 24 : PIECE - 24 + TOPK]
    return mixed, d_tokens, d_gates, g_gate, g_up, g_down


def local(tokens, cotangent, w_gate, w_up, w_down, expert_ids, gates):
    every, across = dispatched(tokens, cotangent, expert_ids, gates)
    count = every.shape[0]
    place, place_t, gate_t, info = pl.pallas_call(
        route_kernel,
        out_shape=[
            of((count, 128), jnp.int32),
            of((8, count), jnp.int32),
            of((8, count), F32),
            of((8 + EXP_GROUP,), jnp.int32),
        ],
        in_specs=[VMEM],
        out_specs=[VMEM, VMEM, VMEM, SMEM],
    )(every)
    return lax.switch(
        info[7],
        [lambda *a, size=size: routed(size, size == SIZES[0], *a) for size in SIZES],
        every,
        across,
        place,
        place_t,
        gate_t,
        info,
        w_gate,
        w_up,
        w_down,
    )


def solution(mesh):
    in_specs = (
        P(("expert", "row"), "col"),
        P(("expert", "row"), "col"),
        P("expert", "col", "row"),
        P("expert", "col", "row"),
        P("expert", "row", "col"),
        P(("expert", "row"), None),
        P(("expert", "row"), None),
    )
    out_specs = (
        P(("expert", "row"), "col"),
        P(("expert", "row"), "col"),
        P(("expert", "row"), None),
        P("expert", "col", "row"),
        P("expert", "col", "row"),
        P("expert", "row", "col"),
    )
    return jax.shard_map(local, mesh=mesh, in_specs=in_specs, out_specs=out_specs, check_vma=False)
```
